32 devices in a mesh: ctx: 8 (over z, y), fsdp: 4 (over x, core).
Axes of the slice: x: 2, y: 2, z: 4, core: 2. Of those that a mesh axis runs over, the one named last changes fastest.
Arguments:
- layer_in: bfloat16 [4, 8192, 1472], P('fsdp', 'ctx'), may hold values from -6 to 6
- out_grad: bfloat16 [4, 8192, 1472], P('fsdp', 'ctx'), may hold values from -6 to 6
- w_query: bfloat16 [1472, 384], P('fsdp'), may hold values from -0.0546875 to 0.0546875
- w_key: bfloat16 [1472, 384], P('fsdp'), may hold values from -0.0546875 to 0.0546875
- w_value: bfloat16 [1472, 384], P('fsdp'), may hold values from -0.15625 to 0.15625
- w_out: bfloat16 [384, 1472], P(None, 'fsdp'), may hold values from -3.59375 to 3.59375
- w_gate: bfloat16 [1472, 3584], P(None, 'fsdp'), may hold values from -0.15625 to 0.15625
- w_up: bfloat16 [1472, 3584], P(None, 'fsdp'), may hold values from -0.15625 to 0.15625
- w_down: bfloat16 [3584, 1472], P('fsdp'), may hold values from -0.09375 to 0.09375
- norm_attn: bfloat16 [1472], P('fsdp'), may hold values from 0.099609375 to 1.8984375
- norm_ffn: bfloat16 [1472], P('fsdp'), may hold values from 0.099609375 to 1.8984375
- rel_bias: bfloat16 [32, 6], P('fsdp'), may hold values from -4 to 4
- deal_table: int32 [128], replicated, may hold values from 0 to 127, as said below
- seg_ids: int32 [4, 4096], P('fsdp'), may hold values from 0 to 7, never falling along the last dimension, each value on 1 to 768 neighbouring positions
Outputs:
- layer_out: bfloat16 [4, 8192, 1472], P('fsdp', 'ctx')
- in_grad: bfloat16 [4, 8192, 1472], P('fsdp', 'ctx')
- grad_query: float32 [1472, 384], P('fsdp')
- grad_key: float32 [1472, 384], P('fsdp')
- grad_value: float32 [1472, 384], P('fsdp')
- grad_out: float32 [384, 1472], P(None, 'fsdp')
- grad_gate: float32 [1472, 3584], P(None, 'fsdp')
- grad_up: float32 [1472, 3584], P(None, 'fsdp')
- grad_down: float32 [3584, 1472], P('fsdp')
- grad_norm_attn: float32 [1472], P('fsdp')
- grad_norm_ffn: float32 [1472], P('fsdp')
- grad_bias: float32 [32, 6], P('fsdp')
The draws below stay inside these ranges and needn't reach their ends.
Inputs may be any that keep to these rules, and one draw needn't show every extreme that they name: deal_table is a permutation of the 128 blocks of a group, the same for all groups.
All inputs are finite; a program needn't handle non-finite values.
Results may differ from the reference program's by a relative error of at most 0.017.
Values may be sent and summed in bfloat16 or wider, within the bound.
A program may use at most 512 MiB of HBM per device.

```python
import math
import jax
import jax.numpy as jnp
import numpy as np
from jax import lax

D = 1472
HEADS = 6
HDIM = 64
FF = 3584
BUCKETS = 32
PROMPT = 4096
CONT = 512
NCONT = 8
BLK = 64
HD = 384
CONTS = 4096
GROUP = 8192
GROUPS = 4
NBLK = 128


def draw_deal_table(key, part):
    half_count = NBLK // 2
    key_order, key_flip = jax.random.split(jax.random.fold_in(key, 17))
    order = jax.random.permutation(key_order, half_count).astype(jnp.int32)
    flips = jax.random.randint(key_flip, (half_count,), 0, 2, dtype=jnp.int32)
    partner = (NBLK - 1 - order).astype(jnp.int32)
    first_slot = jnp.where(flips == 1, partner, order)
    second_slot = jnp.where(flips == 1, order, partner)
    return jnp.stack([first_slot, second_slot], axis=1).reshape(NBLK).astype(jnp.int32)


def steps_of(rng, dims, cuts, low, top_value):
    level = 1.0
    for position, shards_of in cuts:
        draws = jax.random.uniform(jax.random.fold_in(jax.random.fold_in(rng, 6), position), (shards_of,), jnp.float32, low / len(cuts), top_value / len(cuts))
        level = level * jnp.repeat(jnp.exp(draws), dims[position] // shards_of).reshape((-1,) + (1,) * (len(dims) - 1 - position))
    return level


def length_profile(count, total, limit, skew):
    loads = [(1 << 20) // math.isqrt(grade ** skew) + 1 for grade in range(2, count + 1)]
    surplus, given = total - limit - (count - 1), [1] * (count - 1)
    while surplus > 0:
        movable = [i for i in range(count - 1) if given[i] < limit]
        mass, budget = sum([loads[i] for i in movable]), surplus
        for i in movable:
            extra = min(limit - given[i], max(1, budget * loads[i] // mass), surplus)
            given[i] = given[i] + extra
            surplus = surplus - extra
    return np.array([limit] + given)


def ragged_sizes(stream_key, count, total, limit, skew):
    if count == 2:
        one = jax.random.randint(stream_key, (), max(1, total - limit), min(limit, total - 1) + 1)
        return jnp.stack([one, total - one])
    tallies = jnp.asarray(length_profile(count, total, limit, skew), jnp.int32)
    twos = (count - 1) // 2
    donor, receiver = tallies[1:1 + 2 * twos:2], tallies[2:2 + 2 * twos:2]
    slack = jnp.minimum(donor - 1, limit - receiver)
    passed = jax.random.randint(jax.random.fold_in(stream_key, 1), (twos,), 0, 1 << 20) % (slack + 1)
    tallies = tallies.at[1:1 + 2 * twos:2].set(donor - passed).at[2:2 + 2 * twos:2].set(receiver + passed)
    return tallies[jax.random.permutation(jax.random.fold_in(stream_key, 2), count)]


def gaussian(rng, shape, spread, reach, cuts=(), kind=jnp.bfloat16):
    loudness = steps_of(rng, shape, cuts, -0.22, 0.18) if cuts else 1.0
    values = jax.random.normal(rng, shape, jnp.float32) * spread * loudness
    return jnp.minimum(jnp.maximum(values, -reach), reach).astype(kind)


def setup_inputs(seed: int = 0) -> dict:
    seeds = jax.random.split(jax.random.key(seed), 15)
    layer_in = gaussian(seeds[0], (GROUPS, GROUP, D), 1.0, 6.0, ((0, 4), (1, 8)))
    out_grad = gaussian(seeds[1], (GROUPS, GROUP, D), 1.0, 6.0, ((0, 4), (1, 8)))
    w_query = gaussian(seeds[2], (D, HD), (8 * D) ** -0.5, 0.0546875, ((0, 4),))
    w_key = gaussian(seeds[3], (D, HD), (8 * D) ** -0.5, 0.0546875, ((0, 4),))
    w_value = gaussian(seeds[4], (D, HD), D ** -0.5, 0.15625, ((0, 4),))
    w_out = gaussian(seeds[5], (HD, D), 0.6, 3.59375, ((1, 4),))
    w_gate = gaussian(seeds[6], (D, FF), D ** -0.5, 0.15625, ((1, 4),))
    w_up = gaussian(seeds[7], (D, FF), D ** -0.5, 0.15625, ((1, 4),))
    w_down = gaussian(seeds[8], (FF, D), FF ** -0.5, 0.09375, ((0, 4),))
    norm_attn = jnp.clip(1.0 + 0.18 * jax.random.normal(seeds[9], (D,), jnp.float32), 0.099609375, 1.8984375).astype(jnp.bfloat16)
    norm_ffn = jnp.clip(1.0 + 0.18 * jax.random.normal(seeds[10], (D,), jnp.float32), 0.099609375, 1.8984375).astype(jnp.bfloat16)
    rel_bias = gaussian(seeds[11], (BUCKETS, HEADS), 1.0, 4.0, ((0, 4),))
    deal_table = draw_deal_table(jax.random.fold_in(seeds[14], 71), 0)
    seg_ids = jax.vmap(lambda own: jnp.searchsorted(jnp.cumsum(ragged_sizes(own, NCONT, CONTS, CONT + CONT // 2, 1)), jnp.arange(CONTS), side="right"))(jax.random.split(seeds[13], GROUPS)).reshape((GROUPS, CONTS)).astype(jnp.int32)
    return {"layer_in": layer_in, "out_grad": out_grad, "w_query": w_query, "w_key": w_key, "w_value": w_value, "w_out": w_out, "w_gate": w_gate, "w_up": w_up, "w_down": w_down, "norm_attn": norm_attn, "norm_ffn": norm_ffn, "rel_bias": rel_bias, "deal_table": deal_table, "seg_ids": seg_ids}


@jax.custom_vjp
def low(v):
    return lax.optimization_barrier(v.astype(jnp.bfloat16)).astype(jnp.float32)

@jax.custom_vjp
def low_back(v):
    return v

def low_keep(v):
    return (low(v), None)

def low_pass(kept, grad):
    return (grad,)

def back_keep(v):
    return (v, None)

def back_low(kept, grad):
    return (low(grad),)
low.defvjp(low_keep, low_pass)
low_back.defvjp(back_keep, back_low)
epsilon = 1e-06
masked_score = -1e+30
thresholds = [math.ceil(16 * 8 ** (step_t / 16)) for step_t in range(1, 16)]

def bucket_of(distance):
    distance = jnp.maximum(distance, 0)
    far_bucket = jnp.full(distance.shape, 16, jnp.int32)
    for threshold in thresholds:
        far_bucket = far_bucket + (distance >= threshold).astype(jnp.int32)
    return jnp.where(distance < 16, distance, far_bucket).astype(jnp.int32)

def layout(deal_table, seg_row):
    row_index = jnp.arange(GROUP, dtype=jnp.int32)
    dealt_pos = (deal_table[row_index // BLK] * BLK + row_index % BLK).astype(jnp.int32)
    is_cont = dealt_pos >= PROMPT
    offset = jnp.clip(dealt_pos - PROMPT, 0, CONTS - 1).astype(jnp.int32)
    labels = jnp.arange(NCONT, dtype=jnp.int32)
    counts = lax.optimization_barrier(jnp.sum((seg_row[:, None] == labels[None, :]).astype(jnp.int32), axis=0)).astype(jnp.int32)
    starts = (jnp.cumsum(counts) - counts).astype(jnp.int32)
    own_seg = seg_row[offset]
    seg_start = lax.optimization_barrier(jnp.sum(jnp.where(own_seg[:, None] == labels[None, :], starts[None, :], 0), axis=1)).astype(jnp.int32)
    segment = jnp.where(is_cont, own_seg, -1).astype(jnp.int32)
    token_pos = jnp.where(is_cont, PROMPT + offset - seg_start, dealt_pos).astype(jnp.int32)
    return (dealt_pos, segment, token_pos)

def rms_norm(row_block, gain_vec):
    return row_block * lax.rsqrt(lax.optimization_barrier(jnp.mean(row_block * row_block, axis=-1, keepdims=True)) + epsilon) * gain_vec

def matmul_hi(left, right):
    return jnp.dot(left, right, precision=lax.Precision.HIGHEST)

def group_forward(params, group_in, layout_rows):
    w_query, w_key, w_value, w_out, w_gate, w_up, w_down, norm_attn, norm_ffn, rel_bias = params
    dealt_pos, segment, token_pos = layout_rows
    normed = low(rms_norm(group_in, norm_attn))
    queries = low(low_back(matmul_hi(normed, w_query)))
    key_rows = low(low_back(matmul_hi(normed, w_key)))
    value_rows = low(low_back(matmul_hi(normed, w_value)))
    block_rows = min(512, GROUP)
    block_count = GROUP // block_rows
    query_blocks = queries.reshape(block_count, block_rows, HEADS, HDIM)
    key_heads = key_rows.reshape(GROUP, HEADS, HDIM)
    value_heads = value_rows.reshape(GROUP, HEADS, HDIM)

    def attend_block(pieces):
        query_blk, pos_blk, seg_blk, tok_blk = pieces
        raw = jnp.einsum('qhd,khd->hqk', query_blk, key_heads, precision=lax.Precision.HIGHEST)
        buckets = bucket_of(tok_blk[:, None] - token_pos[None, :])
        bias = jnp.transpose(rel_bias[buckets], (2, 0, 1))
        scores = low_back(raw + bias)
        allowed = (dealt_pos[None, :] <= pos_blk[:, None]) & ((dealt_pos[None, :] < PROMPT) | (segment[None, :] == seg_blk[:, None]))
        scores = jnp.where(allowed[None], scores, masked_score)
        row_max = lax.optimization_barrier(jnp.max(scores, axis=-1, keepdims=True))
        shifted = jnp.exp(scores - row_max)
        probs = low(shifted / lax.optimization_barrier(jnp.sum(shifted, axis=-1, keepdims=True)))
        return jnp.einsum('hqk,khd->qhd', probs, value_heads, precision=lax.Precision.HIGHEST)
    attended = lax.map(jax.checkpoint(attend_block), (query_blocks, dealt_pos.reshape(block_count, block_rows), segment.reshape(block_count, block_rows), token_pos.reshape(block_count, block_rows)))
    attended = low(low_back(attended.reshape(GROUP, HEADS * HDIM)))
    mid_rows = group_in + low_back(matmul_hi(attended, w_out))
    normed_ffn = low(rms_norm(mid_rows, norm_ffn))
    gate_pre = low_back(matmul_hi(normed_ffn, w_gate))
    up_pre = low_back(matmul_hi(normed_ffn, w_up))
    hidden = low(jax.nn.gelu(gate_pre, approximate=True) * up_pre)
    return mid_rows + low_back(matmul_hi(hidden, w_down))

def reference(layer_in, out_grad, w_query, w_key, w_value, w_out, w_gate, w_up, w_down, norm_attn, norm_ffn, rel_bias, deal_table, seg_ids):
    params = tuple((weight.astype(jnp.float32) for weight in (w_query, w_key, w_value, w_out, w_gate, w_up, w_down, norm_attn, norm_ffn, rel_bias)))

    def group_step(totals, pieces):
        group_in, group_grad, seg_row = pieces
        layout_rows = layout(deal_table, seg_row)

        def forward(rows_in, weights):
            return group_forward(weights, rows_in, layout_rows)
        result, pullback = jax.vjp(forward, group_in.astype(jnp.float32), params)
        d_rows, d_params = pullback(group_grad.astype(jnp.float32))
        totals = tuple((acc_sum + part for acc_sum, part in zip(totals, d_params)))
        return (totals, (result.astype(jnp.bfloat16), d_rows.astype(jnp.bfloat16)))
    zero_sums = tuple((jnp.zeros_like(weight) for weight in params))
    totals, (layer_out, in_grad) = lax.scan(group_step, zero_sums, (layer_in, out_grad, seg_ids))
    return (layer_out, in_grad, totals[0], totals[1], totals[2], totals[3], totals[4], totals[5], totals[6], totals[7], totals[8], totals[9])
```

```python
import functools
import math

import jax
import jax.numpy as jnp
from jax import lax
from jax.experimental import pallas as pl
from jax.experimental.pallas import tpu as pltpu
from jax.sharding import Mesh, PartitionSpec as P

HEADS = 6
HDIM = 64
PROMPT = 4096
NCONT = 8
BLK = 64
CONTS = 4096
GROUP = 8192
NBLK = GROUP // BLK
PBLK = PROMPT // BLK
LOG2E = 1.4426950408889634
NEG = -3e30
M_INIT = -1e30
WIN = 3
WK = WIN * BLK
FARB = 8
FK = FARB * BLK
thresholds = [math.ceil(16 * 8 ** (step_t / 16)) for step_t in range(1, 16)]
epsilon = 1e-06
BF = jnp.bfloat16
F32 = jnp.float32


def dot_nt(a, b):
    return lax.dot_general(a, b, (((1,), (1,)), ((), ())), preferred_element_type=F32)


def dot_nn(a, b):
    return lax.dot_general(a, b, (((1,), (0,)), ((), ())), preferred_element_type=F32)


def dot_tn(a, b):
    return lax.dot_general(a, b, (((0,), (0,)), ((), ())), preferred_element_type=F32)


class Tab:
    def __init__(self, n):
        self.src = 0
        self.slot = NBLK
        self.blk = NBLK + n
        self.nch = NBLK + 2 * n
        self.zf = NBLK + 3 * n
        self.lim = NBLK + 4 * n
        self.size = NBLK + 5 * n


def lane(shape):
    return lax.broadcasted_iota(jnp.int32, shape, len(shape) - 1)


def sub(shape):
    return lax.broadcasted_iota(jnp.int32, shape, len(shape) - 2)


def stack_super(src, dst, base, hi_c):
    low = lane((BLK, 128)) < 64
    for j in range(4):
        blk = src[base + j]
        pair, one = blk[:, :128], blk[:, 128:]
        zero = jnp.zeros_like(pair)
        u, r = j // 2, (j % 2) * 128
        dst[u, r : r + 64, :] = jnp.where(low, pair, zero)
        dst[u, r + 64 : r + 128, :] = jnp.where(low, zero, pair)
        dst[2, j * 64 : (j + 1) * 64, :] = jnp.where(low, zero, one) if hi_c else jnp.where(low, one, zero)


def near_setup(tab, t, base, z_ref, oo_ref, bias_a, bias_c, oh):
    low = lane((WK, 128)) < 64
    for j in range(4):
        oh[j] = (sub((128, 128)) == oo_ref[base + j]).astype(BF)
    zsum = [lambda x, h=h: dot_nn(z_ref[0, h], x) + dot_nn(z_ref[1, h], x) for h in range(3)]
    for j in range(4):
        bias_a[1, j] = jnp.where(low, zsum[0](oh[j]), zsum[1](oh[j]))
    for p in range(2):
        ohc = jnp.where(lane((128, 128)) < 64, oh[2 * p], oh[2 * p + 1])
        bias_c[1, p] = zsum[2](ohc)


def near_scalars(tab, t, base, i):
    offs, act = [], []
    for j in range(4):
        b = tab[t.blk + base + j]
        off = jnp.where(i == 0, b, jnp.where(i == 1, PBLK - WIN + 2, b - WIN * (i - 1)))
        active = i < tab[t.nch + base + j]
        offs.append(jnp.where(active, off, 2))
        act.append(active)
    return offs, act


def near_low(lo_ref, base, j, i, act):
    lo = lo_ref[base + j]
    lo = jnp.where(i == 1, jnp.zeros_like(lo), lo)
    return jnp.where(act[j], lo, jnp.full_like(lo, 1 << 20))


def far_mask(tab, t, base, u, c, shape):
    pos = c * FK + sub(shape)
    ln = lane(shape)
    if u < 2:
        lim = jnp.where(ln < 128, tab[t.lim + base + 2 * u], tab[t.lim + base + 2 * u + 1])
    else:
        lim = jnp.where(
            ln < 128,
            jnp.where(ln < 64, tab[t.lim + base], tab[t.lim + base + 1]),
            jnp.where(ln < 192, tab[t.lim + base + 2], tab[t.lim + base + 3]),
        )
    return pos < lim


def far_counts(tab, t, base):
    lims = [tab[t.lim + base + j] for j in range(4)]
    least = jnp.minimum(jnp.minimum(lims[0], lims[1]), jnp.minimum(lims[2], lims[3]))
    most = jnp.maximum(jnp.maximum(lims[0], lims[1]), jnp.maximum(lims[2], lims[3]))
    return least // FK, (most + FK - 1) // FK


def near_count(tab, t, base):
    ns = [tab[t.nch + base + j] for j in range(4)]
    return jnp.maximum(jnp.maximum(ns[0], ns[1]), jnp.maximum(ns[2], ns[3]))


def load_sorted(tab, t, n, pairs, kv_hbm, kv, sems):
    def kv_start(p, carry):
        pltpu.make_async_copy(kv_hbm.at[tab[t.src + p]], kv.at[p + 2], sems.at[0]).start()
        return carry

    lax.fori_loop(0, NBLK, kv_start, 0)
    for which, (src, dst) in enumerate(pairs):
        def start(r, carry, src=src, dst=dst, which=which):
            pltpu.make_async_copy(src.at[tab[t.slot + r]], dst.at[r], sems.at[which + 1]).start()
            return carry

        lax.fori_loop(0, n, start, 0)
    pltpu.make_async_copy(kv_hbm, kv.at[pl.ds(2, NBLK)], sems.at[0]).wait()
    for which, (src, dst) in enumerate(pairs):
        pltpu.make_async_copy(src, dst, sems.at[which + 1]).wait()


def k_lanes(u):
    return (0, 128) if u < 2 else (256, 384)


def v_lanes(u):
    return (128, 256) if u < 2 else (256, 384)


def flat(x):
    return x.reshape(x.shape[0] * x.shape[1], x.shape[2])


def transpose_far(kv, dst, lanes):
    def step(c, carry):
        for which, (a, b) in enumerate(lanes):
            x = flat(kv[pl.ds(2 + c * FARB, FARB), :, a:b])
            dst[which, :, pl.ds(pl.multiple_of(c * FK, FK), FK)] = jnp.transpose(x)
        return carry

    lax.fori_loop(0, PROMPT // FK, step, 0)


def fwd_kernel(n, tab, kv_hbm, q_hbm, t_ref, z_ref, lo_ref, oo_ref, o_ref, lse_ref,
               kv, qs, qst, vt, bias_a, bias_c, oh, m, l, acc, sems):
    t = Tab(n)
    kv[0:2] = jnp.zeros((2, BLK, 384), BF)
    load_sorted(tab, t, n, [(q_hbm, qs)], kv_hbm, kv, sems)
    transpose_far(kv, vt, [(128, 256), (256, 384)])
    for j in range(4):
        bias_a[0, j] = t_ref[0]
        bias_a[2, j] = jnp.zeros((WK, 128), F32)
    for p in range(2):
        bias_c[0, p] = t_ref[1]
        bias_c[2, p] = jnp.zeros((WK, 128), F32)

    def update(u, a, b, s, pv):
        m_old = m[u, :, a:b]
        m_new = jnp.maximum(m_old, jnp.max(s, axis=0, keepdims=True))
        p = jnp.exp2(s - m_new)
        alpha = jnp.exp2(m_old - m_new)
        m[u, :, a:b] = m_new
        l[u, :, a:b] = l[u, :, a:b] * alpha + jnp.sum(p, axis=0, keepdims=True)
        acc[u, :, a:b] = acc[u, :, a:b] * alpha + pv(p.astype(BF))

    def super_tile(s_i, carry):
        base = s_i * 4
        stack_super(qs, qst, base, False)
        m[...] = jnp.full(m.shape, M_INIT, F32)
        l[...] = jnp.zeros(l.shape, F32)
        acc[...] = jnp.zeros(acc.shape, F32)
        n_near = near_count(tab, t, base)

        @pl.when(n_near > 1)
        def _():
            near_setup(tab, t, base, z_ref, oo_ref, bias_a, bias_c, oh)

        def near(i, carry):
            offs, act = near_scalars(tab, t, base, i)
            kind = jnp.minimum(i, 2)
            low = lane((WK, 128)) < 64
            for j in range(4):
                u, a = j // 2, (j % 2) * 128
                k = flat(kv[pl.ds(offs[j], WIN), :, 0:128])
                v = flat(kv[pl.ds(offs[j], WIN), :, 128:256])
                s = dot_nt(k, qst[u, a : a + 128, :]) * LOG2E + bias_a[kind, j]
                pos = (offs[j] - 2) * BLK + sub((WK, 128))
                s = jnp.where(pos >= near_low(lo_ref, base, j, i, act), s, NEG)
                update(u, a, a + 128, s, lambda p, v=v: dot_tn(v, p))
            for pr in range(2):
                a = pr * 128
                j0, j1 = 2 * pr, 2 * pr + 1
                x0 = flat(kv[pl.ds(offs[j0], WIN), :, 256:384])
                x1 = flat(kv[pl.ds(offs[j1], WIN), :, 256:384])
                q = qst[2, a : a + 128, :]
                s = jnp.where(low, dot_nt(x0, q), dot_nt(x1, q)) * LOG2E + bias_c[kind, pr]
                half = lane((1, 128)) < 64
                pos0 = jnp.where(half, (offs[j0] - 2) * BLK, (offs[j1] - 2) * BLK)
                lows = jnp.where(
                    half, near_low(lo_ref, base, j0, i, act), near_low(lo_ref, base, j1, i, act)
                )
                s = jnp.where(sub((WK, 128)) >= lows - pos0, s, NEG)
                update(
                    2, a, a + 128, s,
                    lambda p, x0=x0, x1=x1: jnp.where(
                        lane((128, 128)) < 64, dot_tn(x0, p), dot_tn(x1, p)
                    ),
                )
            return carry

        lax.fori_loop(0, n_near, near, 0)

        def far(masked, c, carry):
            for u in range(3):
                a, b = k_lanes(u)
                k = flat(kv[pl.ds(2 + c * FARB, FARB), :, a:b])
                s = dot_nt(k, qst[u]) * LOG2E
                if masked:
                    s = jnp.where(far_mask(tab, t, base, u, c, s.shape), s, NEG)
                v = vt[u // 2, :, pl.ds(pl.multiple_of(c * FK, FK), FK)]
                update(u, 0, 256, s, lambda p, v=v: dot_nn(v, p))
            return carry

        n_full, n_far = far_counts(tab, t, base)
        lax.fori_loop(0, n_full, functools.partial(far, False), 0)
        lax.fori_loop(n_full, n_far, functools.partial(far, True), 0)
        low = lane((BLK, 128)) < 64
        for u in range(3):
            lse_ref[s_i, u] = m[u] + jnp.log(l[u]) * LOG2E
            o = jnp.transpose(acc[u] / l[u])
            if u < 2:
                for k in range(2):
                    r = k * 128
                    slot = tab[t.slot + base + 2 * u + k]
                    o_ref[slot, :, 0:128] = jnp.where(low, o[r : r + 64], o[r + 64 : r + 128]).astype(BF)
            else:
                for j in range(4):
                    slot = tab[t.slot + base + j]
                    piece = o[j * 64 : (j + 1) * 64]
                    o_ref[slot, :, 128:256] = jnp.where(low, jnp.zeros_like(piece), piece).astype(BF)
        return carry

    lax.fori_loop(0, n // 4, super_tile, 0)


def bwd_kernel(n, tab, kv_hbm, q_hbm, do_hbm, at_hbm, t_ref, z_ref, lo_ref, oo_ref, lse_ref,
               dq_ref, dkv_hbm, gt_ref, gz_ref,
               kv, dkv, qs, dos, ats, qst, dst, qcm, dcm, kt, bias_a, bias_c, oh, ga, gc, dq, delta, sems):
    t = Tab(n)
    kv[0:2] = jnp.zeros((2, BLK, 384), BF)
    load_sorted(tab, t, n, [(q_hbm, qs), (do_hbm, dos), (at_hbm, ats)], kv_hbm, kv, sems)
    transpose_far(kv, kt, [(0, 128), (256, 384)])

    def clear(p, carry):
        dkv[p] = jnp.zeros((BLK, 384), F32)
        return carry

    lax.fori_loop(0, NBLK + 2, clear, 0)
    for j in range(4):
        bias_a[0, j] = t_ref[0]
        bias_a[2, j] = jnp.zeros((WK, 128), F32)
    for p in range(2):
        bias_c[0, p] = t_ref[1]
        bias_c[2, p] = jnp.zeros((WK, 128), F32)
    ga[...] = jnp.zeros(ga.shape, F32)
    gc[...] = jnp.zeros(gc.shape, F32)
    gz_ref[...] = jnp.zeros(gz_ref.shape, F32)

    def add_rows(first, count, a, b, val):
        dkv[pl.ds(first, count), :, a:b] += val.reshape(count, BLK, b - a)

    def super_tile(s_i, carry):
        base = s_i * 4
        stack_super(qs, qst, base, False)
        stack_super(dos, dst, base, True)
        half_rows = sub((128, 128)) < 64
        for pr in range(2):
            q = qst[2, pr * 128 : (pr + 1) * 128, :]
            d = dst[2, pr * 128 : (pr + 1) * 128, :]
            for k in range(2):
                keep = half_rows if k == 0 else jnp.logical_not(half_rows)
                qcm[pr, k] = jnp.where(keep, q, jnp.zeros_like(q))
                dcm[pr, k] = jnp.where(keep, d, jnp.zeros_like(d))
        prods = []
        for j in range(4):
            prods.append(dos[base + j].astype(F32) * ats[base + j].astype(F32))
        low = lane((BLK, 128)) < 64
        zero = jnp.zeros((BLK, 128), F32)
        for u in range(2):
            parts = []
            for k in range(2):
                pair = prods[2 * u + k][:, :128]
                parts += [jnp.where(low, pair, zero), jnp.where(low, zero, pair)]
            stacked = jnp.concatenate(parts, axis=0)
            delta[u] = jnp.sum(jnp.transpose(stacked), axis=0, keepdims=True)
        stacked = jnp.concatenate([jnp.where(low, zero, pr[:, 128:]) for pr in prods], axis=0)
        delta[2] = jnp.sum(jnp.transpose(stacked), axis=0, keepdims=True)
        dq[...] = jnp.zeros(dq.shape, F32)
        n_near = near_count(tab, t, base)

        @pl.when(n_near > 1)
        def _():
            near_setup(tab, t, base, z_ref, oo_ref, bias_a, bias_c, oh)

        def near(i, carry):
            offs, act = near_scalars(tab, t, base, i)
            kind = jnp.minimum(i, 2)
            low = lane((WK, 128)) < 64
            for j in range(4):
                u, a = j // 2, (j % 2) * 128
                k = flat(kv[pl.ds(offs[j], WIN), :, 0:128])
                v = flat(kv[pl.ds(offs[j], WIN), :, 128:256])
                q = qst[u, a : a + 128, :]
                d = dst[u, a : a + 128, :]
                s = dot_nt(k, q) * LOG2E + bias_a[kind, j]
                pos = (offs[j] - 2) * BLK + sub((WK, 128))
                s = jnp.where(pos >= near_low(lo_ref, base, j, i, act), s, NEG)
                p = jnp.exp2(s - lse_ref[s_i, u, :, a : a + 128])
                ds = (p * (dot_nt(v, d) - delta[u, :, a : a + 128])).astype(BF)
                add_rows(offs[j], WIN, 0, 128, dot_nn(ds, q))
                add_rows(offs[j], WIN, 128, 256, dot_nn(p.astype(BF), d))
                dq[u, :, a : a + 128] += dot_tn(k, ds)
                slot = jnp.where(i == 0, 0, jnp.where(i == 1, 1 + j, 5))
                ga[slot] += ds.astype(F32)
            for pr in range(2):
                a = pr * 128
                j0, j1 = 2 * pr, 2 * pr + 1
                x0 = flat(kv[pl.ds(offs[j0], WIN), :, 256:384])
                x1 = flat(kv[pl.ds(offs[j1], WIN), :, 256:384])
                q = qst[2, a : a + 128, :]
                d = dst[2, a : a + 128, :]
                s = jnp.where(low, dot_nt(x0, q), dot_nt(x1, q)) * LOG2E + bias_c[kind, pr]
                half = lane((1, 128)) < 64
                pos0 = jnp.where(half, (offs[j0] - 2) * BLK, (offs[j1] - 2) * BLK)
                lows = jnp.where(
                    half, near_low(lo_ref, base, j0, i, act), near_low(lo_ref, base, j1, i, act)
                )
                s = jnp.where(sub((WK, 128)) >= lows - pos0, s, NEG)
                p = jnp.exp2(s - lse_ref[s_i, 2, :, a : a + 128])
                dp = jnp.where(low, dot_nt(x0, d), dot_nt(x1, d))
                ds = (p * (dp - delta[2, :, a : a + 128])).astype(BF)
                pb = p.astype(BF)
                for k, jj in enumerate((j0, j1)):
                    add_rows(offs[jj], WIN, 256, 384, dot_nn(ds, qcm[pr, k]) + dot_nn(pb, dcm[pr, k]))
                dq[2, :, a : a + 128] += jnp.where(
                    lane((128, 128)) < 64, dot_tn(x0, ds), dot_tn(x1, ds)
                )
                slot = jnp.where(i == 0, 0, jnp.where(i == 1, 1 + pr, 3))
                gc[slot] += ds.astype(F32)
            return carry

        lax.fori_loop(0, n_near, near, 0)

        @pl.when(n_near > 1)
        def _():
            half = lane((128, 128)) < 64
            none = jnp.zeros((128, 128), BF)
            for j in range(4):
                g = ga[1 + j].astype(BF)
                gz_ref[0] += dot_nt(g, jnp.where(half, oh[j], none))
                gz_ref[1] += dot_nt(g, jnp.where(half, none, oh[j]))
                ga[1 + j] = jnp.zeros((WK, 128), F32)
            for pr in range(2):
                g = gc[1 + pr].astype(BF)
                gz_ref[2] += dot_nt(g, jnp.where(half, oh[2 * pr], oh[2 * pr + 1]))
                gc[1 + pr] = jnp.zeros((WK, 128), F32)

        def far(masked, c, carry):
            first = 2 + c * FARB
            for u in range(3):
                a, b = k_lanes(u)
                k = flat(kv[pl.ds(first, FARB), :, a:b])
                s = dot_nt(k, qst[u]) * LOG2E
                if masked:
                    s = jnp.where(far_mask(tab, t, base, u, c, s.shape), s, NEG)
                p = jnp.exp2(s - lse_ref[s_i, u])
                va, vb = v_lanes(u)
                v = k if u == 2 else flat(kv[pl.ds(first, FARB), :, va:vb])
                ds = (p * (dot_nt(v, dst[u]) - delta[u])).astype(BF)
                pb = p.astype(BF)
                if u < 2:
                    add_rows(first, FARB, a, b, dot_nn(ds, qst[u]))
                    add_rows(first, FARB, va, vb, dot_nn(pb, dst[u]))
                else:
                    add_rows(first, FARB, a, b, dot_nn(ds, qst[u]) + dot_nn(pb, dst[u]))
                dq[u] += dot_nn(kt[u // 2, :, pl.ds(pl.multiple_of(c * FK, FK), FK)], ds)
            return carry

        n_full, n_far = far_counts(tab, t, base)
        lax.fori_loop(0, n_full, functools.partial(far, False), 0)
        lax.fori_loop(n_full, n_far, functools.partial(far, True), 0)
        for u in range(3):
            o = jnp.transpose(dq[u])
            if u < 2:
                for k in range(2):
                    r = k * 128
                    slot = tab[t.slot + base + 2 * u + k]
                    dq_ref[slot, :, 0:128] = jnp.where(low, o[r : r + 64], o[r + 64 : r + 128]).astype(BF)
            else:
                for j in range(4):
                    slot = tab[t.slot + base + j]
                    piece = o[j * 64 : (j + 1) * 64]
                    dq_ref[slot, :, 128:256] = jnp.where(low, piece, jnp.zeros_like(piece)).astype(BF)
        return carry

    lax.fori_loop(0, n // 4, super_tile, 0)
    gt_ref[0] = ga[0]
    gt_ref[1] = gc[0]

    def give(p, carry):
        kv[p + 2] = dkv[p + 2].astype(BF)
        pltpu.make_async_copy(kv.at[p + 2], dkv_hbm.at[tab[t.src + p]], sems.at[0]).start()
        return carry

    lax.fori_loop(0, NBLK, give, 0)
    pltpu.make_async_copy(kv.at[pl.ds(2, NBLK)], dkv_hbm, sems.at[0]).wait()


VM = pl.BlockSpec(memory_space=pltpu.VMEM)
HB = pl.BlockSpec(memory_space=pl.ANY)
SM = pl.BlockSpec(memory_space=pltpu.SMEM)


def attn_fwd(tab, kv, q, t_tab, z_tab, lo, oo):
    n = q.shape[0]
    pairs = n * BLK * 2600 * 3
    return pl.pallas_call(
        functools.partial(fwd_kernel, n),
        out_shape=(
            jax.ShapeDtypeStruct((n, BLK, 256), BF),
            jax.ShapeDtypeStruct((n // 4, 3, 1, 256), F32),
        ),
        in_specs=[SM, HB, HB, VM, VM, VM, VM],
        out_specs=(VM, VM),
        scratch_shapes=[
            pltpu.VMEM((NBLK + 2, BLK, 384), BF),
            pltpu.VMEM((n, BLK, 256), BF),
            pltpu.VMEM((3, 256, 128), BF),
            pltpu.VMEM((2, 128, PROMPT), BF),
            pltpu.VMEM((3, 4, WK, 128), F32),
            pltpu.VMEM((3, 2, WK, 128), F32),
            pltpu.VMEM((4, 128, 128), BF),
            pltpu.VMEM((3, 1, 256), F32),
            pltpu.VMEM((3, 1, 256), F32),
            pltpu.VMEM((3, 128, 256), F32),
            pltpu.SemaphoreType.DMA((2,)),
        ],
        compiler_params=pltpu.CompilerParams(vmem_limit_bytes=36 << 20),
        cost_estimate=pl.CostEstimate(
            flops=pairs * 1024, bytes_accessed=8 << 20, transcendentals=pairs
        ),
        name="attn_fwd",
    )(tab, kv, q, t_tab, z_tab, lo, oo)


def attn_bwd(tab, kv, q, do, at, t_tab, z_tab, lo, oo, lse):
    n = q.shape[0]
    pairs = n * BLK * 2600 * 3
    return pl.pallas_call(
        functools.partial(bwd_kernel, n),
        out_shape=(
            jax.ShapeDtypeStruct((n, BLK, 256), BF),
            jax.ShapeDtypeStruct((NBLK, BLK, 384), BF),
            jax.ShapeDtypeStruct((2, WK, 128), F32),
            jax.ShapeDtypeStruct((3, WK, 128), F32),
        ),
        in_specs=[SM, HB, HB, HB, HB, VM, VM, VM, VM, VM],
        out_specs=(VM, HB, VM, VM),
        scratch_shapes=[
            pltpu.VMEM((NBLK + 2, BLK, 384), BF),
            pltpu.VMEM((NBLK + 2, BLK, 384), F32),
            pltpu.VMEM((n, BLK, 256), BF),
            pltpu.VMEM((n, BLK, 256), BF),
            pltpu.VMEM((n, BLK, 256), BF),
            pltpu.VMEM((3, 256, 128), BF),
            pltpu.VMEM((3, 256, 128), BF),
            pltpu.VMEM((2, 2, 128, 128), BF),
            pltpu.VMEM((2, 2, 128, 128), BF),
            pltpu.VMEM((2, 128, PROMPT), BF),
            pltpu.VMEM((3, 4, WK, 128), F32),
            pltpu.VMEM((3, 2, WK, 128), F32),
            pltpu.VMEM((4, 128, 128), BF),
            pltpu.VMEM((6, WK, 128), F32),
            pltpu.VMEM((4, WK, 128), F32),
            pltpu.VMEM((3, 128, 256), F32),
            pltpu.VMEM((3, 1, 256), F32),
            pltpu.SemaphoreType.DMA((4,)),
        ],
        compiler_params=pltpu.CompilerParams(vmem_limit_bytes=52 << 20),
        cost_estimate=pl.CostEstimate(
            flops=pairs * 2560, bytes_accessed=16 << 20, transcendentals=pairs
        ),
        name="attn_bwd",
    )(tab, kv, q, do, at, t_tab, z_tab, lo, oo, lse)


def bucket_of(distance):
    distance = jnp.maximum(distance, 0)
    far_bucket = jnp.full(distance.shape, 16, jnp.int32)
    for threshold in thresholds:
        far_bucket = far_bucket + (distance >= threshold).astype(jnp.int32)
    return jnp.where(distance < 16, distance, far_bucket)


def near_distance():
    diag = (WIN - 1) * BLK + jnp.arange(BLK)[None, :] - jnp.arange(WK)[:, None]
    tail = WK + jnp.arange(128)[None, :] - jnp.arange(WK)[:, None]
    return diag.astype(jnp.int32), tail.astype(jnp.int32)


def bias_tables(table):
    last = table.shape[0] - 1
    rel = (table - table[last:]) * LOG2E
    diag, tail = near_distance()

    def pick(dist):
        bucket = bucket_of(dist)
        out = jnp.zeros((3,) + dist.shape, F32)
        for b in range(last):
            out = jnp.where(bucket[None] == b, rel[b][:, None, None], out)
        return out

    d = jnp.where(diag[None] >= 0, pick(diag), NEG)
    z = pick(tail)
    t_tab = jnp.stack([jnp.concatenate([d[0], d[1]], axis=1), jnp.concatenate([d[2], d[2]], axis=1)])
    z_hi = z.astype(BF)
    z_lo = (z - z_hi.astype(F32)).astype(BF)
    return t_tab, jnp.stack([z_hi, z_lo])


def bias_grads(gt, gz, buckets):
    diag, tail = near_distance()
    gd = jnp.stack([gt[0, :, :64], gt[0, :, 64:], gt[1, :, :64] + gt[1, :, 64:]])
    bd, bt = bucket_of(diag), bucket_of(tail)
    labels = jnp.arange(buckets - 1, dtype=jnp.int32)[:, None, None, None]
    seen = diag >= 0
    one = jnp.sum(jnp.where((bd[None, None] == labels) & seen[None, None], gd[None], 0.0), axis=(2, 3))
    two = jnp.sum(jnp.where(bt[None, None] == labels, gz[None], 0.0), axis=(2, 3))
    near = one + two
    return jnp.concatenate([near, -jnp.sum(near, axis=0, keepdims=True)], axis=0)


def plan(deal_table, seg_row, ctx, nb):
    n = 2 * nb
    par = ctx % 2
    slot = jnp.arange(NBLK, dtype=jnp.int32)
    owner = slot // nb
    where_kv = ((owner // 2) * 2 + (owner % 2 + par) % 2) * nb + slot % nb
    src = jnp.sum(jnp.where(deal_table[None, :] == slot[:, None], where_kv[None, :], 0), axis=1)
    own = lax.dynamic_slice_in_dim(deal_table, ctx * nb, nb)
    other = lax.dynamic_slice_in_dim(deal_table, (ctx + 1 - 2 * par) * nb, nb)
    rb = jnp.concatenate([own, other])
    rank = jnp.sum((rb[None, :] < rb[:, None]).astype(jnp.int32), axis=1)
    pos = jnp.arange(n, dtype=jnp.int32)
    pick = (rank[None, :] == pos[:, None]).astype(jnp.int32)
    rslot = jnp.sum(pick * pos[None, :], axis=1)
    rblk = jnp.sum(pick * rb[None, :], axis=1)
    labels = jnp.arange(NCONT, dtype=jnp.int32)
    starts = jnp.sum((seg_row[None, :] < labels[:, None]).astype(jnp.int32), axis=1)
    cpos = rblk[:, None] * BLK + jnp.arange(BLK, dtype=jnp.int32)[None, :] - PROMPT
    ss = jnp.max(jnp.where(starts[None, None, :] <= cpos[:, :, None], starts[None, None, :], 0), axis=2)
    is_cont = rblk >= PBLK
    lo = jnp.where(is_cont[:, None], PROMPT + ss, 0)
    oo = jnp.where(is_cont[:, None], jnp.minimum(cpos - ss, 127), 127)
    first = (PROMPT + ss[:, 0]) // BLK
    more = jnp.maximum(rblk - (WIN - 1) - first, 0)
    nch = jnp.where(is_cont, 2 + (more + WIN - 1) // WIN, 1)
    zf = jnp.zeros_like(nch)
    lim = jnp.where(is_cont, PROMPT - WK, jnp.maximum(rblk - (WIN - 1), 0) * BLK)
    tab = jnp.concatenate([src, rslot, rblk, nch, zf, lim]).astype(jnp.int32)
    dup = lambda x: jnp.concatenate([x, x], axis=1)[:, None, :].astype(jnp.int32)
    return tab, dup(lo), dup(oo)


def rms_norm(row_block, gain_vec):
    return (
        row_block
        * lax.rsqrt(jnp.mean(row_block * row_block, axis=-1, keepdims=True) + epsilon)
        * gain_vec
    )


def gelu_mix(gate_pre, up_pre):
    return jax.nn.gelu(gate_pre, approximate=True) * up_pre


def head_cols(w, h):
    return w[:, h * HDIM : (h + 1) * HDIM]


def swap(x, axis):
    return lax.ppermute(x, axis, [(0, 1), (1, 0)])


def pick_half(par, even, odd):
    return jnp.where(par == 0, even, odd)


def on_device(
    layer_in, out_grad, w_query, w_key, w_value, w_out, w_gate, w_up, w_down,
    norm_attn, norm_ffn, rel_bias, deal_table, seg_ids,
):
    _, rows, width = layer_in.shape
    nb = rows // BLK
    cz, par = lax.axis_index("cz"), lax.axis_index("cy")
    steps = lax.axis_size("cz")
    ctx = cz * 2 + par
    share = w_query.shape[0]
    fs = ("fx", "fc")
    cs = ("cz", "cy")
    shards = width // share

    none = jnp.zeros((share, HDIM), BF)
    out_t = jnp.transpose(w_out)
    packs, outs = [], []
    for p in range(2):
        a, b, c = 3 * p, 3 * p + 1, 3 * p + 2
        packs.append(jnp.concatenate(
            [head_cols(w_key, a), head_cols(w_key, b), head_cols(w_value, a), head_cols(w_value, b),
             head_cols(w_key, c), head_cols(w_value, c), head_cols(w_query, a), head_cols(w_query, b),
             head_cols(w_query, c)], axis=1))
        outs.append(jnp.concatenate(
            [head_cols(out_t, a), head_cols(out_t, b), none, head_cols(out_t, c)], axis=1))
    extra = jnp.zeros((share, HDIM), BF)
    extra = jnp.concatenate(
        [norm_attn[:, None], norm_ffn[:, None],
         jnp.pad(rel_bias, ((0, share - rel_bias.shape[0]), (0, 0))),
         jnp.zeros((share, HDIM - 2 - HEADS), BF)], axis=1)
    w_qkv = jnp.concatenate(
        [pick_half(par, packs[0], packs[1]), extra, pick_half(par, packs[1], packs[0]), none], axis=1)
    w_o = jnp.concatenate([pick_half(par, outs[0], outs[1]), pick_half(par, outs[1], outs[0])], axis=1)
    w_qkv = lax.all_gather(w_qkv, fs, axis=0, tiled=True)
    w_o = lax.all_gather(w_o, fs, axis=0, tiled=True)
    gain_attn = w_qkv[:, 576].astype(F32)
    gain_ffn = w_qkv[:, 577].astype(F32)
    bias_rows = rel_bias.shape[0]
    table = w_qkv.reshape(shards, share, 1280)[:, :bias_rows, 578 : 578 + HEADS]
    table = table.reshape(shards * bias_rows, HEADS).astype(F32)
    my_table = pick_half(par, table[:, :3], table[:, 3:])

    def spread(w):
        far = swap(w, "fx")
        return [w, swap(w, "fc"), far, swap(far, "fc")]

    gates, ups, downs = spread(w_gate), spread(w_up), spread(w_down)

    rows_in = layer_in.reshape(rows, width).astype(F32)
    normed = rms_norm(rows_in, gain_attn).astype(BF)
    qkv = jnp.dot(normed, w_qkv, preferred_element_type=F32).astype(BF)
    mine, other = qkv[:, :640], swap(qkv[:, 640:], "cy")
    kv = jnp.stack([mine[:, :384], other[:, :384]])
    q = jnp.stack([mine[:, 384:], other[:, 384:]]).reshape(2 * nb, BLK, 256)
    kv = lax.all_gather(kv, "cz", axis=0, tiled=True).reshape(NBLK, BLK, 384)
    tab, lo, oo = plan(deal_table, seg_ids[0], ctx, nb)
    t_tab, z_tab = bias_tables(my_table)
    att, lse = attn_fwd(tab, kv, q, t_tab, z_tab, lo, oo)
    halves = att.reshape(2, rows, 256)
    att_rows = jnp.concatenate([halves[0], swap(halves[1], "cy")], axis=1)

    mid = rows_in + dot_nt(att_rows, w_o)
    normed_ffn = rms_norm(mid, gain_ffn).astype(BF)
    dy = out_grad.reshape(rows, width)
    total, d_ffn_in = mid, None
    parts = []
    for r in range(4):
        gate_pre = jnp.dot(normed_ffn, gates[r], preferred_element_type=F32)
        up_pre = jnp.dot(normed_ffn, ups[r], preferred_element_type=F32)
        hidden, mix_back = jax.vjp(gelu_mix, gate_pre, up_pre)
        hidden = hidden.astype(BF)
        total = total + jnp.dot(hidden, downs[r], preferred_element_type=F32)
        d_gate, d_up = mix_back(dot_nt(dy, downs[r]))
        d_gate, d_up = d_gate.astype(BF), d_up.astype(BF)
        back = dot_nt(d_gate, gates[r]) + dot_nt(d_up, ups[r])
        d_ffn_in = back if d_ffn_in is None else d_ffn_in + back
        parts.append((dot_tn(normed_ffn, d_gate), dot_tn(normed_ffn, d_up), dot_tn(hidden, dy)))
    layer_out = total.astype(BF).reshape(layer_in.shape)

    def fold(g):
        near = g[0] + swap(g[1].astype(BF), "fc").astype(F32)
        far = g[2] + swap(g[3].astype(BF), "fc").astype(F32)
        return near + swap(far.astype(BF), "fx").astype(F32)

    def over_ctx(g):
        piece = lax.psum_scatter(g.astype(BF), cs, scatter_dimension=0, tiled=True)
        return lax.all_gather(piece, cs, axis=0, tiled=True).astype(F32)

    grad_gate, grad_up, grad_down = [over_ctx(fold([p[k] for p in parts])) for k in range(3)]

    _, norm_back_ffn = jax.vjp(rms_norm, mid, gain_ffn)
    d_mid_norm, g_gain_ffn = norm_back_ffn(d_ffn_in)
    d_mid = dy.astype(F32) + d_mid_norm
    d_branch = d_mid.astype(BF)
    d_att = jnp.dot(d_branch, w_o, preferred_element_type=F32).astype(BF)
    do = jnp.stack([d_att[:, :256], swap(d_att[:, 256:], "cy")]).reshape(2 * nb, BLK, 256)
    g_out = dot_tn(d_branch, att_rows)
    dq, dkv, gt, gz = attn_bwd(tab, kv, q, do, att, t_tab, z_tab, lo, oo, lse)
    dq = dq.reshape(2, rows, 256)
    dq_other = swap(dq[1], "cy")
    dkv = lax.psum_scatter(dkv.reshape(GROUP, 384), "cz", scatter_dimension=0, tiled=True)
    dkv_other = swap(dkv[rows:], "cy")
    d_qkv = jnp.concatenate([dkv[:rows], dq[0], dkv_other, dq_other], axis=1)
    g_qkv = dot_tn(normed, d_qkv)
    d_normed = dot_nt(d_qkv, w_qkv)
    _, norm_back_attn = jax.vjp(rms_norm, rows_in, gain_attn)
    d_in_norm, g_gain_attn = norm_back_attn(d_normed)
    in_grad = (d_mid + d_in_norm).astype(BF).reshape(layer_in.shape)

    f_here = lax.axis_index("fx") * 2 + lax.axis_index("fc")

    def reduce_attn(g):
        half = g.shape[1] // 2
        g = pick_half(par, g, jnp.concatenate([g[:, half:], g[:, :half]], axis=1))
        blocks = g.reshape(shards, share, g.shape[1])
        away = lambda r: lax.dynamic_index_in_dim(blocks, f_here ^ r, keepdims=False)
        own = fold([away(r) for r in range(4)])
        pad = (-share) % 64
        return over_ctx(jnp.pad(own, ((0, pad), (0, 0))))[:share]

    g_out = reduce_attn(g_out)
    g_qkv = reduce_attn(g_qkv)
    cols = lambda g, at: g[:, at : at + HDIM]
    p0, p1 = 0, 640
    grad_key = jnp.concatenate([cols(g_qkv, p + o) for p in (p0, p1) for o in (0, 64, 256)], axis=1)
    grad_value = jnp.concatenate([cols(g_qkv, p + o) for p in (p0, p1) for o in (128, 192, 320)], axis=1)
    grad_query = jnp.concatenate([cols(g_qkv, p + o) for p in (p0, p1) for o in (384, 448, 512)], axis=1)
    grad_out = jnp.transpose(
        jnp.concatenate([cols(g_out, p + o) for p in (0, 256) for o in (0, 64, 192)], axis=1))

    g_bias = bias_grads(gt, gz, table.shape[0])
    zero = jnp.zeros_like(g_bias)
    g_bias = jnp.concatenate([pick_half(par, g_bias, zero), pick_half(par, zero, g_bias)], axis=1)
    small = lax.psum((g_gain_attn, g_gain_ffn, g_bias), cs + fs)
    own = lambda v, size: lax.dynamic_slice_in_dim(v, f_here * size, size)
    return (
        layer_out, in_grad, grad_query, grad_key, grad_value, grad_out, grad_gate, grad_up, grad_down,
        own(small[0], share), own(small[1], share), own(small[2], bias_rows),
    )


def solution(mesh):
    devices = mesh.devices
    ctx_size, fsdp_size = mesh.shape["ctx"], mesh.shape["fsdp"]
    split = Mesh(devices.reshape(ctx_size // 2, 2, fsdp_size // 2, 2), ("cz", "cy", "fx", "fc"))
    cs, fs = ("cz", "cy"), ("fx", "fc")
    in_specs = (
        P(fs, cs, None), P(fs, cs, None), P(fs, None), P(fs, None), P(fs, None), P(None, fs),
        P(None, fs), P(None, fs), P(fs, None), P(fs), P(fs), P(fs, None), P(), P(fs, None),
    )
    out_specs = (
        P(fs, cs, None), P(fs, cs, None), P(fs, None), P(fs, None), P(fs, None), P(None, fs),
        P(None, fs), P(None, fs), P(fs, None), P(fs), P(fs), P(fs, None),
    )
    return jax.shard_map(
        on_device, mesh=split, in_specs=in_specs, out_specs=out_specs, check_vma=False
    )
```

```python
import functools
import math

import jax
import jax.numpy as jnp
from jax import lax
from jax.experimental import pallas as pl
from jax.experimental.pallas import tpu as pltpu
from jax.sharding import Mesh, PartitionSpec as P

HEADS = 6
HDIM = 64
PROMPT = 4096
NCONT = 8
BLK = 64
CONTS = 4096
GROUP = 8192
NBLK = GROUP // BLK
PBLK = PROMPT // BLK
LOG2E = 1.4426950408889634
NEG = -3e30
M_INIT = -1e30
WIN = 3
WK = WIN * BLK
FARB = 16
FK = FARB * BLK
thresholds = [math.ceil(16 * 8 ** (step_t / 16)) for step_t in range(1, 16)]
epsilon = 1e-06
BF = jnp.bfloat16
F32 = jnp.float32
HINT = 1 << 20


def dot_nt(a, b):
    return lax.dot_general(a, b, (((1,), (1,)), ((), ())), preferred_element_type=F32)


def dot_nn(a, b):
    return lax.dot_general(a, b, (((1,), (0,)), ((), ())), preferred_element_type=F32)


def dot_tn(a, b):
    return lax.dot_general(a, b, (((0,), (0,)), ((), ())), preferred_element_type=F32)


class Tab:
    def __init__(self, n):
        self.src = 0
        self.slot = NBLK
        self.blk = NBLK + n
        self.nch = NBLK + 2 * n
        self.zf = NBLK + 3 * n
        self.lim = NBLK + 4 * n
        self.size = NBLK + 5 * n


def lane(shape):
    return lax.broadcasted_iota(jnp.int32, shape, len(shape) - 1)


def sub(shape):
    return lax.broadcasted_iota(jnp.int32, shape, len(shape) - 2)


def stack_super(tab, t, src, dst, base, one, hi):
    low = lane((BLK, 128)) < 64
    for j in range(4):
        blk = src[tab[t.slot + base + j]]
        zero = jnp.zeros_like(blk)
        if one:
            dst[0, j * 64 : (j + 1) * 64, :] = jnp.where(low, zero, blk) if hi else jnp.where(low, blk, zero)
        else:
            u, r = j // 2, (j % 2) * 128
            dst[u, r : r + 64, :] = jnp.where(low, blk, zero)
            dst[u, r + 64 : r + 128, :] = jnp.where(low, zero, blk)


def near_parts(one):
    return [(0, 0), (0, 128)] if one else [(0, 0), (0, 128), (1, 0), (1, 128)]


def near_setup(base, one, z_ref, oo_ref, bias, oh):
    low = lane((WK, 128)) < 64
    for j in range(4):
        oh[j] = (sub((128, 128)) == oo_ref[base + j]).astype(BF)
    spread = lambda h, x: dot_nn(z_ref[0, h], x) + dot_nn(z_ref[1, h], x)
    if one:
        for p in range(2):
            bias[1, p] = spread(0, jnp.where(lane((128, 128)) < 64, oh[2 * p], oh[2 * p + 1]))
    else:
        for j in range(4):
            bias[1, j] = jnp.where(low, spread(0, oh[j]), spread(1, oh[j]))


def near_scalars(tab, t, base, i):
    offs, act = [], []
    for j in range(4):
        b = tab[t.blk + base + j]
        off = jnp.where(i == 0, b - (WIN - 1), jnp.where(i == 1, PBLK - WIN, b - (WIN - 1) - WIN * (i - 1)))
        active = i < tab[t.nch + base + j]
        offs.append(jnp.where(active, off, 0))
        act.append(active)
    return offs, act


def near_low(lo_ref, base, j, i, act):
    lo = lo_ref[base + j]
    lo = jnp.where(i == 1, jnp.zeros_like(lo), lo)
    return jnp.where(act[j], lo, jnp.full_like(lo, 1 << 20))


def near_keep(lo_ref, base, one, x, i, act, offs):
    edge = lambda j: near_low(lo_ref, base, j, i, act) - offs[j] * BLK
    if one:
        return sub((WK, 128)) >= jnp.where(lane((1, 128)) < 64, edge(2 * x), edge(2 * x + 1))
    return sub((WK, 128)) >= edge(x)


def near_dot(kv, wins, one, x, a, b, q):
    if one:
        left, right = [dot_nt(rows_of(kv, wins[2 * x + k], a, b), q) for k in range(2)]
        return jnp.where(lane(left.shape) < 64, left, right)
    return dot_nt(rows_of(kv, wins[x], a, b), q)


def near_dot_t(kv, wins, one, x, a, b, p):
    if one:
        left, right = [dot_tn(rows_of(kv, wins[2 * x + k], a, b), p) for k in range(2)]
        return jnp.where(lane(left.shape) < 64, left, right)
    return dot_tn(rows_of(kv, wins[x], a, b), p)


def near_scores(kv, qst, bias, lo_ref, base, one, i, offs, act, wins):
    kind = jnp.minimum(i, 2)
    out = []
    for x, (u, a) in enumerate(near_parts(one)):
        s = near_dot(kv, wins, one, x, 0, 128, qst[u, a : a + 128, :]) * LOG2E + bias[kind, x]
        out.append(jnp.where(near_keep(lo_ref, base, one, x, i, act, offs), s, NEG))
    return out


def far_mask(tab, t, base, one, u, c, shape):
    pos = c * FK + sub(shape)
    ln = lane(shape)
    lim = lambda j: tab[t.lim + base + j]
    if one:
        low = jnp.where(ln < 64, lim(0), lim(1))
        return pos < jnp.where(ln < 128, low, jnp.where(ln < 192, lim(2), lim(3)))
    return pos < jnp.where(ln < 128, lim(2 * u), lim(2 * u + 1))


def far_counts(tab, t, base):
    lims = [tab[t.lim + base + j] for j in range(4)]
    least = jnp.minimum(jnp.minimum(lims[0], lims[1]), jnp.minimum(lims[2], lims[3]))
    most = jnp.maximum(jnp.maximum(lims[0], lims[1]), jnp.maximum(lims[2], lims[3]))
    return least // FK, (most + FK - 1) // FK


def near_count(tab, t, base):
    ns = [tab[t.nch + base + j] for j in range(4)]
    return jnp.maximum(jnp.maximum(ns[0], ns[1]), jnp.maximum(ns[2], ns[3]))


def blocks_of(tab, t, first, count):
    return [tab[t.src + jnp.maximum(first + i, 0)] for i in range(count)]


def rows_of(ref, blocks, a, b):
    return jnp.concatenate([ref[i, :, a:b] for i in blocks], axis=0)


def transpose_far(tab, t, kv, dst, a, b):
    def step(c, carry):
        x = rows_of(kv, blocks_of(tab, t, c * FARB, FARB), a, b)
        dst[:, pl.ds(pl.multiple_of(c * FK, FK), FK)] = jnp.transpose(x)
        return carry

    lax.fori_loop(0, PROMPT // FK, step, 0)


def start_bias(t_ref, bias):
    for x in range(bias.shape[1]):
        bias[0, x] = t_ref[...]
        bias[2, x] = jnp.zeros((WK, 128), F32)


def give_rows(tab, t, base, one, u, val, dst, hi):
    low = lane((BLK, 128)) < 64
    if one:
        for j in range(4):
            piece = val[j * 64 : (j + 1) * 64]
            zero = jnp.zeros_like(piece)
            dst[tab[t.slot + base + j]] = (jnp.where(low, zero, piece) if hi else jnp.where(low, piece, zero)).astype(BF)
    else:
        for k in range(2):
            r = k * 128
            dst[tab[t.slot + base + 2 * u + k]] = jnp.where(low, val[r : r + 64], val[r + 64 : r + 128]).astype(BF)


def fwd_kernel(n, one, tab, kv, qs, t_ref, z_ref, lo_ref, oo_ref, o_ref, lse_ref, qst, vt, bias, oh, m, l, acc):
    t = Tab(n)
    units = 1 if one else 2
    va, vb = (0, 128) if one else (128, 256)
    transpose_far(tab, t, kv, vt, va, vb)
    start_bias(t_ref, bias)

    def update(at, ss, pv):
        olds = [m[u, :, a:b] for u, a, b in at]
        news = [jnp.maximum(old, jnp.max(s, axis=0, keepdims=True)) for old, s in zip(olds, ss)]
        ps = [jnp.exp2(s - new) for s, new in zip(ss, news)]
        al = [jnp.exp2(old - new) for old, new in zip(olds, news)]
        sums = [jnp.sum(p, axis=0, keepdims=True) for p in ps]
        outs = [pv(x, p.astype(BF)) for x, p in enumerate(ps)]
        for x, (u, a, b) in enumerate(at):
            m[u, :, a:b] = news[x]
            l[u, :, a:b] = l[u, :, a:b] * al[x] + sums[x]
            acc[u, :, a:b] = acc[u, :, a:b] * al[x] + outs[x]

    def super_tile(s_i, carry):
        base = s_i * 4
        stack_super(tab, t, qs, qst, base, one, False)
        m[...] = jnp.full(m.shape, M_INIT, F32)
        l[...] = jnp.zeros(l.shape, F32)
        acc[...] = jnp.zeros(acc.shape, F32)
        n_near = near_count(tab, t, base)

        @pl.when(n_near > 1)
        def _():
            near_setup(base, one, z_ref, oo_ref, bias, oh)

        def near(i, carry):
            offs, act = near_scalars(tab, t, base, i)
            wins = [blocks_of(tab, t, off, WIN) for off in offs]
            ss = near_scores(kv, qst, bias, lo_ref, base, one, i, offs, act, wins)
            at = [(u, a, a + 128) for u, a in near_parts(one)]
            update(at, ss, lambda x, p: near_dot_t(kv, wins, one, x, va, vb, p))
            return carry

        lax.fori_loop(0, n_near, near, 0)

        def far(masked, c, carry):
            k = rows_of(kv, blocks_of(tab, t, c * FARB, FARB), 0, 128)
            ss = [dot_nt(k, qst[u]) * LOG2E for u in range(units)]
            if masked:
                ss = [jnp.where(far_mask(tab, t, base, one, u, c, s.shape), s, NEG) for u, s in enumerate(ss)]
            v = vt[:, pl.ds(pl.multiple_of(c * FK, FK), FK)]
            update([(u, 0, 256) for u in range(units)], ss, lambda x, p: dot_nn(v, p))
            return carry

        n_full, n_far = far_counts(tab, t, base)
        lax.fori_loop(0, n_full, functools.partial(far, False), 0)
        lax.fori_loop(n_full, n_far, functools.partial(far, True), 0)
        for u in range(units):
            lse_ref[s_i, u] = m[u] + jnp.log(l[u]) * LOG2E
            give_rows(tab, t, base, one, u, jnp.transpose(acc[u] / l[u]), o_ref, True)
        return carry

    lax.fori_loop(0, n // 4, super_tile, 0)


def bwd_kernel(n, one, tab, kv, qs, dos, ats, t_ref, z_ref, lo_ref, oo_ref, lse_ref,
               dq_ref, dkv_ref, gt_ref, gz_ref, dkv, qst, dst, qm, dm, kt, bias, oh, gn, dq, delta):
    t = Tab(n)
    units = 1 if one else 2
    va, vb = (0, 128) if one else (128, 256)
    parts = near_parts(one)
    transpose_far(tab, t, kv, kt, 0, 128)
    start_bias(t_ref, bias)

    def clear(p, carry):
        dkv[p] = jnp.zeros(dkv.shape[1:], F32)
        return carry

    lax.fori_loop(0, NBLK, clear, 0)
    gn[...] = jnp.zeros(gn.shape, F32)
    gz_ref[...] = jnp.zeros(gz_ref.shape, F32)

    def add_rows(blocks, a, b, val):
        for i, block in enumerate(blocks):
            dkv[block, :, a:b] += val[i * BLK : (i + 1) * BLK]

    def super_tile(s_i, carry):
        base = s_i * 4
        stack_super(tab, t, qs, qst, base, one, False)
        stack_super(tab, t, dos, dst, base, one, True)
        if one:
            half_rows = sub((128, 128)) < 64
            for x in range(2):
                for src, dst_m in ((qst, qm), (dst, dm)):
                    val = src[0, x * 128 : (x + 1) * 128, :]
                    zero = jnp.zeros_like(val)
                    dst_m[x, 0] = jnp.where(half_rows, val, zero)
                    dst_m[x, 1] = jnp.where(half_rows, zero, val)
        low = lane((BLK, 128)) < 64
        zero = jnp.zeros((BLK, 128), F32)
        prods = []
        for j in range(4):
            slot = tab[t.slot + base + j]
            prods.append(dos[slot].astype(F32) * ats[slot].astype(F32))
        for u in range(units):
            if one:
                stacked = [jnp.where(low, zero, p) for p in prods]
            else:
                stacked = [x for p in prods[2 * u : 2 * u + 2] for x in (jnp.where(low, p, zero), jnp.where(low, zero, p))]
            delta[u] = jnp.sum(jnp.transpose(jnp.concatenate(stacked, axis=0)), axis=0, keepdims=True)
        dq[...] = jnp.zeros(dq.shape, F32)
        n_near = near_count(tab, t, base)

        @pl.when(n_near > 1)
        def _():
            near_setup(base, one, z_ref, oo_ref, bias, oh)

        def near(i, carry):
            offs, act = near_scalars(tab, t, base, i)
            wins = [blocks_of(tab, t, off, WIN) for off in offs]
            ss = near_scores(kv, qst, bias, lo_ref, base, one, i, offs, act, wins)
            dps = [near_dot(kv, wins, one, x, va, vb, dst[u, a : a + 128, :]) for x, (u, a) in enumerate(parts)]
            ps = [jnp.exp2(s - lse_ref[s_i, u, :, a : a + 128]) for s, (u, a) in zip(ss, parts)]
            ds = [(p * (dp - delta[u, :, a : a + 128])).astype(BF) for p, dp, (u, a) in zip(ps, dps, parts)]
            pb = [p.astype(BF) for p in ps]
            dqs = [near_dot_t(kv, wins, one, x, 0, 128, ds[x]) for x in range(len(parts))]
            adds = []
            for x, (u, a) in enumerate(parts):
                if one:
                    for k in range(2):
                        adds.append((wins[2 * x + k], 0, 128, dot_nn(ds[x], qm[x, k]) + dot_nn(pb[x], dm[x, k])))
                else:
                    adds.append((wins[x], 0, 128, dot_nn(ds[x], qst[u, a : a + 128, :])))
                    adds.append((wins[x], va, vb, dot_nn(pb[x], dst[u, a : a + 128, :])))
            for add in adds:
                add_rows(*add)
            for x, (u, a) in enumerate(parts):
                slot = jnp.where(i == 0, 0, jnp.where(i == 1, 1 + x, 1 + len(parts)))
                gn[slot] += ds[x].astype(F32)
                dq[u, :, a : a + 128] += dqs[x]
            return carry

        lax.fori_loop(0, n_near, near, 0)

        @pl.when(n_near > 1)
        def _():
            half = lane((128, 128)) < 64
            none = jnp.zeros((128, 128), BF)
            for x in range(len(parts)):
                g = gn[1 + x].astype(BF)
                if one:
                    gz_ref[0] += dot_nt(g, jnp.where(half, oh[2 * x], oh[2 * x + 1]))
                else:
                    gz_ref[0] += dot_nt(g, jnp.where(half, oh[x], none))
                    gz_ref[1] += dot_nt(g, jnp.where(half, none, oh[x]))
                gn[1 + x] = jnp.zeros((WK, 128), F32)

        def far(masked, c, carry):
            blocks = blocks_of(tab, t, c * FARB, FARB)
            k = rows_of(kv, blocks, 0, 128)
            v = k if one else rows_of(kv, blocks, va, vb)
            ss = [dot_nt(k, qst[u]) * LOG2E for u in range(units)]
            dps = [dot_nt(v, dst[u]) for u in range(units)]
            if masked:
                ss = [jnp.where(far_mask(tab, t, base, one, u, c, s.shape), s, NEG) for u, s in enumerate(ss)]
            ps = [jnp.exp2(s - lse_ref[s_i, u]) for u, s in enumerate(ss)]
            ds = [(p * (dp - delta[u])).astype(BF) for u, (p, dp) in enumerate(zip(ps, dps))]
            pb = [p.astype(BF) for p in ps]
            if one:
                add_rows(blocks, 0, 128, dot_nn(ds[0], qst[0]) + dot_nn(pb[0], dst[0]))
            else:
                add_rows(blocks, 0, 128, dot_nn(ds[0], qst[0]) + dot_nn(ds[1], qst[1]))
                add_rows(blocks, va, vb, dot_nn(pb[0], dst[0]) + dot_nn(pb[1], dst[1]))
            for u in range(units):
                dq[u] += dot_nn(kt[:, pl.ds(pl.multiple_of(c * FK, FK), FK)], ds[u])
            return carry

        n_full, n_far = far_counts(tab, t, base)
        lax.fori_loop(0, n_full, functools.partial(far, False), 0)
        lax.fori_loop(n_full, n_far, functools.partial(far, True), 0)
        for u in range(units):
            give_rows(tab, t, base, one, u, jnp.transpose(dq[u]), dq_ref, False)
        return carry

    lax.fori_loop(0, n // 4, super_tile, 0)
    gt_ref[...] = gn[0]

    def give(p, carry):
        dkv_ref[p] = dkv[p].astype(BF)
        return carry

    lax.fori_loop(0, NBLK, give, 0)


VM = pl.BlockSpec(memory_space=pltpu.VMEM)
HB = pl.BlockSpec(memory_space=pl.ANY)
SM = pl.BlockSpec(memory_space=pltpu.SMEM)


def attn_fwd(one, tab, kv, q, t_tab, z_tab, lo, oo):
    n = q.shape[0]
    units, parts = (1, 2) if one else (2, 4)
    return pl.pallas_call(
        functools.partial(fwd_kernel, n, one),
        out_shape=(
            jax.ShapeDtypeStruct((n, BLK, 128), BF),
            jax.ShapeDtypeStruct((n // 4, units, 1, 256), F32),
        ),
        in_specs=[SM] + [VM] * 6,
        out_specs=(VM, VM),
        scratch_shapes=[
            pltpu.VMEM((units, 256, 128), BF),
            pltpu.VMEM((128, PROMPT), BF),
            pltpu.VMEM((3, parts, WK, 128), F32),
            pltpu.VMEM((4, 128, 128), BF),
            pltpu.VMEM((units, 1, 256), F32),
            pltpu.VMEM((units, 1, 256), F32),
            pltpu.VMEM((units, 128, 256), F32),
        ],
        compiler_params=pltpu.CompilerParams(vmem_limit_bytes=30 << 20),
        cost_estimate=pl.CostEstimate(flops=HINT, bytes_accessed=HINT, transcendentals=0),
        name="attn_fwd_one" if one else "attn_fwd_two",
    )(tab, kv, q, t_tab, z_tab, lo, oo)


def attn_bwd(one, tab, kv, q, do, at, t_tab, z_tab, lo, oo, lse):
    n = q.shape[0]
    units, parts = (1, 2) if one else (2, 4)
    lanes = kv.shape[2]
    masked = (2, 2, 128, 128) if one else (1, 1, 16, 128)
    return pl.pallas_call(
        functools.partial(bwd_kernel, n, one),
        out_shape=(
            jax.ShapeDtypeStruct((n, BLK, 128), BF),
            jax.ShapeDtypeStruct((NBLK, BLK, lanes), BF),
            jax.ShapeDtypeStruct((WK, 128), F32),
            jax.ShapeDtypeStruct((units, WK, 128), F32),
        ),
        in_specs=[SM] + [VM] * 9,
        out_specs=(VM, VM, VM, VM),
        scratch_shapes=[
            pltpu.VMEM((NBLK, BLK, lanes), F32),
            pltpu.VMEM((units, 256, 128), BF),
            pltpu.VMEM((units, 256, 128), BF),
            pltpu.VMEM(masked, BF),
            pltpu.VMEM(masked, BF),
            pltpu.VMEM((128, PROMPT), BF),
            pltpu.VMEM((3, parts, WK, 128), F32),
            pltpu.VMEM((4, 128, 128), BF),
            pltpu.VMEM((2 + parts, WK, 128), F32),
            pltpu.VMEM((units, 128, 256), F32),
            pltpu.VMEM((units, 1, 256), F32),
        ],
        compiler_params=pltpu.CompilerParams(vmem_limit_bytes=44 << 20),
        cost_estimate=pl.CostEstimate(flops=HINT, bytes_accessed=HINT, transcendentals=0),
        name="attn_bwd_one" if one else "attn_bwd_two",
    )(tab, kv, q, do, at, t_tab, z_tab, lo, oo, lse)


def bucket_of(distance):
    distance = jnp.maximum(distance, 0)
    far_bucket = jnp.full(distance.shape, 16, jnp.int32)
    for threshold in thresholds:
        far_bucket = far_bucket + (distance >= threshold).astype(jnp.int32)
    return jnp.where(distance < 16, distance, far_bucket)


def near_distance():
    diag = (WIN - 1) * BLK + jnp.arange(BLK)[None, :] - jnp.arange(WK)[:, None]
    tail = WK + jnp.arange(128)[None, :] - jnp.arange(WK)[:, None]
    return diag.astype(jnp.int32), tail.astype(jnp.int32)


def bias_tables(table):
    last = table.shape[0] - 1
    rel = (table - table[last:]) * LOG2E
    diag, tail = near_distance()

    def pick(dist):
        bucket = bucket_of(dist)
        out = jnp.zeros((3,) + dist.shape, F32)
        for b in range(last):
            out = jnp.where(bucket[None] == b, rel[b][:, None, None], out)
        return out

    d = jnp.where(diag[None] >= 0, pick(diag), NEG)
    z = pick(tail)
    two, one = jnp.concatenate([d[0], d[1]], axis=1), jnp.concatenate([d[2], d[2]], axis=1)
    z_hi = z.astype(BF)
    z_lo = (z - z_hi.astype(F32)).astype(BF)
    z = jnp.stack([z_hi, z_lo])
    return (two, z[:, :2]), (one, z[:, 2:])


def bias_grads(gt_two, gz_two, gt_one, gz_one, buckets):
    diag, tail = near_distance()
    gd = jnp.stack([gt_two[:, :64], gt_two[:, 64:], gt_one[:, :64] + gt_one[:, 64:]])
    gz = jnp.concatenate([gz_two, gz_one])
    bd, bt = bucket_of(diag), bucket_of(tail)
    labels = jnp.arange(buckets - 1, dtype=jnp.int32)[:, None, None, None]
    seen = diag >= 0
    one = jnp.sum(jnp.where((bd[None, None] == labels) & seen[None, None], gd[None], 0.0), axis=(2, 3))
    two = jnp.sum(jnp.where(bt[None, None] == labels, gz[None], 0.0), axis=(2, 3))
    near = one + two
    return jnp.concatenate([near, -jnp.sum(near, axis=0, keepdims=True)], axis=0)


def plan(deal_table, seg_row, ctx, nb):
    n = 2 * nb
    par = ctx % 2
    slot = jnp.arange(NBLK, dtype=jnp.int32)
    owner = slot // nb
    where_kv = ((owner // 2) * 2 + (owner % 2 + par) % 2) * nb + slot % nb
    src = jnp.sum(jnp.where(deal_table[None, :] == slot[:, None], where_kv[None, :], 0), axis=1)
    own = lax.dynamic_slice_in_dim(deal_table, ctx * nb, nb)
    other = lax.dynamic_slice_in_dim(deal_table, (ctx + 1 - 2 * par) * nb, nb)
    rb = jnp.concatenate([own, other])
    rank = jnp.sum((rb[None, :] < rb[:, None]).astype(jnp.int32), axis=1)
    pos = jnp.arange(n, dtype=jnp.int32)
    pick = (rank[None, :] == pos[:, None]).astype(jnp.int32)
    rslot = jnp.sum(pick * pos[None, :], axis=1)
    rblk = jnp.sum(pick * rb[None, :], axis=1)
    labels = jnp.arange(NCONT, dtype=jnp.int32)
    starts = jnp.sum((seg_row[None, :] < labels[:, None]).astype(jnp.int32), axis=1)
    cpos = rblk[:, None] * BLK + jnp.arange(BLK, dtype=jnp.int32)[None, :] - PROMPT
    ss = jnp.max(jnp.where(starts[None, None, :] <= cpos[:, :, None], starts[None, None, :], 0), axis=2)
    is_cont = rblk >= PBLK
    lo = jnp.where(is_cont[:, None], PROMPT + ss, 0)
    oo = jnp.where(is_cont[:, None], jnp.minimum(cpos - ss, 127), 127)
    first = (PROMPT + ss[:, 0]) // BLK
    more = jnp.maximum(rblk - (WIN - 1) - first, 0)
    nch = jnp.where(is_cont, 2 + (more + WIN - 1) // WIN, 1)
    zf = jnp.zeros_like(nch)
    lim = jnp.where(is_cont, PROMPT - WK, jnp.maximum(rblk - (WIN - 1), 0) * BLK)
    tab = jnp.concatenate([src, rslot, rblk, nch, zf, lim]).astype(jnp.int32)
    dup = lambda x: jnp.concatenate([x, x], axis=1)[:, None, :].astype(jnp.int32)
    return tab, dup(lo), dup(oo)


def gelu_parts(v):
    c = math.sqrt(2 / math.pi)
    sq = v * v
    th = jnp.tanh(c * v * (1 + 0.044715 * sq))
    half = 0.5 * (1 + th)
    return v * half, half + 0.5 * c * v * (1 - th * th) * (1 + 3 * 0.044715 * sq)


def ffn_kernel(h, dy, wga, wgb, wua, wub, wda, wdb, hida, hidb, dga, dgb, dua, dub, *g_refs):
    rows = h.shape[1]
    step = min(256, rows)
    w_in = jnp.transpose(jnp.concatenate([wga[...], wgb[...], wua[...], wub[...]], axis=1))
    w_down = jnp.transpose(jnp.concatenate([wda[...], wdb[...]], axis=1))
    for r in range(0, rows, step):
        both = dot_nn(w_in, h[:, r : r + step])
        d_hidden = dot_nn(w_down, dy[:, r : r + step])
        gate, up = both[:256], both[256:]
        act, slope = gelu_parts(gate)
        for a, b, val in ((hida, hidb, act * up), (dga, dgb, d_hidden * up * slope), (dua, dub, d_hidden * act)):
            val = val.astype(BF)
            a[:, r : r + step] = val[:128]
            b[:, r : r + step] = val[128:]
    for k, (left, a, b) in enumerate(((h, dga, dgb), (h, dua, dub), (dy, hida, hidb))):
        g = dot_nt(left[...], jnp.concatenate([a[...], b[...]], axis=0)).astype(BF)
        g_refs[k][...] = g[:, :128]
        g_refs[k + 3][...] = g[:, 128:]


def ffn_pair(h, dy, gates, ups, downs):
    width, rows = h.shape
    units = gates[0].shape[1]
    whole = pl.BlockSpec((width, rows), lambda i: (0, 0), pipeline_mode=pl.Buffered(1))
    col = pl.BlockSpec((width, 128), lambda i: (0, i))
    act = pl.BlockSpec((128, rows), lambda i: (i, 0))
    return pl.pallas_call(
        ffn_kernel,
        grid=(units // 128,),
        out_shape=[jax.ShapeDtypeStruct((units, rows), BF)] * 6 + [jax.ShapeDtypeStruct((width, units), BF)] * 6,
        in_specs=[whole, whole] + [col] * 6,
        out_specs=[act] * 6 + [col] * 6,
        compiler_params=pltpu.CompilerParams(vmem_limit_bytes=44 << 20),
        cost_estimate=pl.CostEstimate(flops=HINT, bytes_accessed=HINT, transcendentals=0),
        name="ffn_pair",
    )(h, dy, *gates, *ups, *downs)


def each(count, body):
    def step(i, carry):
        body(i)
        return carry

    lax.fori_loop(0, count, step, 0)


def norm_back(x_at, d_at, gain, g_gain, rows, give):
    width = gain.shape[0]
    part = width // 8
    feats = [slice(f * part, (f + 1) * part) for f in range(8)]
    cols = min(256, rows)
    g_gain[...] = jnp.zeros(g_gain.shape, F32)

    def body(i):
        at = pl.ds(pl.multiple_of(i * cols, cols), cols)
        sq = jnp.zeros((1, cols), F32)
        dot = jnp.zeros((1, cols), F32)
        for f in feats:
            x = x_at[f, at].astype(F32)
            sq = sq + jnp.sum(x * x, axis=0, keepdims=True)
            dot = dot + jnp.sum(d_at[f, at] * gain[f, :] * x, axis=0, keepdims=True)
        rs = lax.rsqrt(sq / width + epsilon)
        coef = rs * rs * rs * dot / width
        for f in feats:
            x, d = x_at[f, at].astype(F32), d_at[f, at]
            give(f, at, rs * (d * gain[f, :]) - x * coef)
            g_gain[f, :] += jnp.sum(d * (x * rs), axis=1, keepdims=True)

    each(rows // cols, body)


def ffn_back_kernel(*refs):
    ds, ws = refs[:8], refs[8:16]
    mid_in, dy_in, gain, w_o_in, d_mid, d_branch, d_att, g_gain, dbuf, wbuf, mid, dy, w_o, acc, sems, late = refs[16:]
    slots = dbuf.shape[0]
    shards = len(ds) // 2

    def copies(i):
        s = i % slots
        return [pltpu.make_async_copy(src[i + k * shards], dst.at[s, k], sems.at[s, w, k])
                for k in range(2) for w, (src, dst) in enumerate(((ds, dbuf), (ws, wbuf)))]

    others = [pltpu.make_async_copy(a, b, late.at[i])
              for i, (a, b) in enumerate(((mid_in, mid), (dy_in, dy), (w_o_in, w_o)))]
    for i in range(slots):
        for c in copies(i):
            c.start()
    for c in others:
        c.start()
    rows = mid.shape[1]
    cols = min(512, rows)

    def add(i, s):
        def body(c):
            at = pl.ds(pl.multiple_of(c * cols, cols), cols)
            part = dot_nn(
                jnp.concatenate([wbuf[s, 0], wbuf[s, 1]], axis=1),
                jnp.concatenate([dbuf[s, 0, :, at], dbuf[s, 1, :, at]], axis=0),
            )
            if i == 0:
                acc[:, at] = part
            else:
                acc[:, at] += part

        each(rows // cols, body)

    for i in range(shards):
        s = i % slots
        for c in copies(i):
            c.wait()
        add(i, s)
        if i + slots < shards:
            for c in copies(i + slots):
                c.start()
    for c in others:
        c.wait()

    def give(f, at, val):
        val = dy[f, at].astype(F32) + val
        d_mid[f, at] = val
        d_branch[f, at] = val.astype(BF)

    norm_back(mid, acc, gain, g_gain, rows, give)

    def out(c):
        at = pl.ds(pl.multiple_of(c * cols, cols), cols)
        d_att[at, :] = dot_tn(d_branch[:, at], w_o[...]).astype(BF)

    each(rows // cols, out)


def ffn_back(d_list, w_list, mid, dy, gain, w_o):
    width, rows = mid.shape
    units = d_list[0].shape[0]
    return pl.pallas_call(
        ffn_back_kernel,
        out_shape=(
            jax.ShapeDtypeStruct((width, rows), F32),
            jax.ShapeDtypeStruct((width, rows), BF),
            jax.ShapeDtypeStruct((rows, w_o.shape[1]), BF),
            jax.ShapeDtypeStruct((width, 1), F32),
        ),
        in_specs=[HB] * 18 + [VM, HB],
        out_specs=(VM, VM, VM, VM),
        scratch_shapes=[
            pltpu.VMEM((2, 2, units, rows), BF),
            pltpu.VMEM((2, 2, width, units), BF),
            pltpu.VMEM((width, rows), F32),
            pltpu.VMEM((width, rows), BF),
            pltpu.VMEM(w_o.shape, BF),
            pltpu.VMEM((width, rows), F32),
            pltpu.SemaphoreType.DMA((2, 2, 2)),
            pltpu.SemaphoreType.DMA((3,)),
        ],
        compiler_params=pltpu.CompilerParams(vmem_limit_bytes=58 << 20),
        cost_estimate=pl.CostEstimate(flops=HINT, bytes_accessed=HINT, transcendentals=0),
        name="ffn_back",
    )(*d_list, *w_list, mid, dy, gain, w_o)


def in_back_kernel(d_qkv, w_qkv, x, h, gain, d_mid, extra, in_grad, g_qkv, acc, g_gain):
    width, rows = x.shape
    cols = min(256, rows)

    def grads(c):
        at = pl.ds(pl.multiple_of(c * 256, 256), 256)
        g_qkv[:, at] = dot_nn(h[...], d_qkv[:, at]).astype(BF)

    each(d_qkv.shape[1] // 256, grads)

    def back(c):
        at = pl.ds(pl.multiple_of(c * cols, cols), cols)
        acc[:, at] = dot_nt(w_qkv[...], d_qkv[at, :])

    each(rows // cols, back)

    def give(f, at, val):
        in_grad[f, at] = (d_mid[f, at] + val).astype(BF)

    norm_back(x, acc, gain, g_gain, rows, give)
    ln = lane((width, 128))
    spare = jnp.where(ln == 64, g_gain[...], extra[...])
    g_qkv[:, 512:640] = jnp.where(ln < 64, g_qkv[:, 512:640].astype(F32), spare).astype(BF)


def in_back(d_qkv, w_qkv, x, h, gain, d_mid, extra):
    width, rows = x.shape
    return pl.pallas_call(
        in_back_kernel,
        out_shape=(
            jax.ShapeDtypeStruct((width, rows), BF),
            jax.ShapeDtypeStruct((width, d_qkv.shape[1]), BF),
        ),
        in_specs=[VM] * 7,
        out_specs=(VM, VM),
        scratch_shapes=[pltpu.VMEM((width, rows), F32), pltpu.VMEM((width, 1), F32)],
        compiler_params=pltpu.CompilerParams(vmem_limit_bytes=56 << 20),
        cost_estimate=pl.CostEstimate(flops=HINT, bytes_accessed=HINT, transcendentals=0),
        name="in_back",
    )(d_qkv, w_qkv, x, h, gain, d_mid, extra)


def pack_kernel(par, w_q, w_k, w_v, w_o, norms, table, qkv_out, o_out):
    low = lane((w_q.shape[0], 128)) < 64
    even = par[0] == 0
    tiles = lambda w: [w[:, i : i + 128].astype(F32) for i in (0, 128, 256)]
    turn = lambda v: pltpu.roll(v, 64, 1)

    def heads(w):
        a, b, c = tiles(w)
        return (a, b, turn(b)), (jnp.where(low, turn(b), turn(c)), turn(c), c)

    def packs(w):
        one, two = heads(w)
        choose = lambda x, y: jnp.where(even, x, y)
        return [tuple(choose(x, y) for x, y in zip(one, two)), tuple(choose(y, x) for x, y in zip(one, two))]

    spare = dot_tn(norms[...], (lane((8, 128)) == sub((8, 128)) + 64).astype(BF))
    pad = jnp.zeros((w_q.shape[0] - table.shape[0], 128), F32)
    spare = spare + jnp.concatenate([table[...], pad], axis=0)
    q, k, v, o = packs(w_q), packs(w_k), packs(w_v), packs(w_o)
    for p in range(2):
        third = jnp.where(low, q[p][1], spare if p == 0 else jnp.zeros_like(spare))
        for i, val in enumerate((k[p][0], v[p][0], q[p][0], jnp.where(low, k[p][1], v[p][2]), third)):
            qkv_out[:, p * 640 + i * 128 : p * 640 + (i + 1) * 128] = val.astype(BF)
        o_out[:, p * 256 : p * 256 + 128] = o[p][0].astype(BF)
        o_out[:, p * 256 + 128 : (p + 1) * 256] = jnp.where(low, jnp.zeros_like(spare), o[p][2]).astype(BF)


def pack(par, w_q, w_k, w_v, w_o, norm_attn, norm_ffn, rel_bias):
    share = w_q.shape[0]
    norms = jnp.pad(jnp.stack([norm_attn, norm_ffn]), ((0, 6), (0, 0)))
    rows = rel_bias.shape[0]
    table = jnp.pad(rel_bias.astype(F32), ((0, (-rows) % 8), (66, 128 - 66 - rel_bias.shape[1])))
    return pl.pallas_call(
        pack_kernel,
        out_shape=(jax.ShapeDtypeStruct((share, 1280), BF), jax.ShapeDtypeStruct((share, 512), BF)),
        in_specs=[SM] + [VM] * 6,
        out_specs=(VM, VM),
        cost_estimate=pl.CostEstimate(flops=HINT, bytes_accessed=HINT, transcendentals=0),
        name="pack",
    )(par.reshape(1), w_q, w_k, w_v, w_o, norms, table)


def swap(x, axis):
    return lax.ppermute(x, axis, [(0, 1), (1, 0)])


def pick_half(par, even, odd):
    return jnp.where(par == 0, even, odd)


def up32(x):
    return x.astype(F32)


def rms_cols(x, gain):
    return x * lax.rsqrt(jnp.mean(x * x, axis=0, keepdims=True) + epsilon) * gain


def after(*values):
    return lax.optimization_barrier(values)


def ctx_bits(cz, par, steps):
    out = [(par, lambda x: swap(x, "cy"))]
    bit = 1
    while bit < steps:
        perm = [(i, i ^ bit) for i in range(steps)]
        out.append(((cz // bit) % 2, lambda x, perm=perm: lax.ppermute(x, "cz", perm)))
        bit *= 2
    return out


def split_by(v, bit):
    half = v.shape[0] // 2
    return pick_half(bit, v[:half], v[half:]), pick_half(bit, v[half:], v[:half])


def ctx_scatter(v, bits):
    for bit, move in bits:
        keep, send = split_by(v, bit)
        v = up32(keep) + up32(move(send.astype(BF)))
    return v.astype(BF)


def ctx_gather(v, bits):
    for bit, move in reversed(bits):
        other = move(v)
        v = jnp.concatenate([pick_half(bit, v, other), pick_half(bit, other, v)])
    return v


def on_device(
    layer_in, out_grad, w_query, w_key, w_value, w_out, w_gate, w_up, w_down,
    norm_attn, norm_ffn, rel_bias, deal_table, seg_ids,
):
    _, rows, width = layer_in.shape
    nb = rows // BLK
    cz, par = lax.axis_index("cz"), lax.axis_index("cy")
    steps = lax.axis_size("cz")
    ctx = cz * 2 + par
    share = w_query.shape[0]
    fs = ("fx", "fc")
    shards = width // share
    bits = ctx_bits(cz, par, steps)

    w_qkv, w_o = pack(par, w_query, w_key, w_value, jnp.transpose(w_out), norm_attn, norm_ffn, rel_bias)
    w_qkv = lax.all_gather(w_qkv, fs, axis=0, tiled=True)
    gain_attn = up32(w_qkv[:, 576:577])
    gain_ffn = up32(w_qkv[:, 577:578])
    bias_rows = rel_bias.shape[0]
    table = w_qkv.reshape(shards, share, 1280)[:, :bias_rows, 578 : 578 + HEADS]
    table = up32(table.reshape(shards * bias_rows, HEADS))
    my_table = pick_half(par, table[:, :3], table[:, 3:])

    own_w = (w_gate, w_up, jnp.transpose(w_down))
    w_qkv, w_o, *sent = after(w_qkv, w_o, *own_w)
    w_o = lax.all_gather(w_o, fs, axis=0, tiled=True)
    quarter = width // 4
    pieces = [swap(sent[2][i * quarter : j * quarter], "fx") for i, j in ((0, 1), (1, 2), (2, 4))]
    far_w = [swap(w, "fx") for w in sent[:2]]

    x = jnp.transpose(layer_in.reshape(rows, width))
    dy = jnp.transpose(out_grad.reshape(rows, width))
    h1 = rms_cols(up32(x), gain_attn).astype(BF)
    qkv = dot_tn(h1, w_qkv).astype(BF)
    two, one = qkv[:, :384], qkv[:, 384:640]
    other, pieces[0] = after(swap(qkv[:, 640:1024], "cy"), pieces[0])
    two = jnp.stack([two, other])
    other, pieces[1] = after(swap(qkv[:, 1024:], "cy"), pieces[1])
    one = jnp.stack([one, other])
    blocks = lambda v: v.reshape(2 * nb, BLK, v.shape[-1])
    gather = lambda v: lax.all_gather(v, "cz", axis=0, tiled=True).reshape(NBLK, BLK, v.shape[-1])
    kv2, q2 = gather(two[:, :, :256]), blocks(two[:, :, 256:])
    kv1, q1 = gather(one[:, :, :128]), blocks(one[:, :, 128:])
    tab, lo, oo = plan(deal_table, seg_ids[0], ctx, nb)
    bias2, bias1 = bias_tables(my_table)
    att2, lse2 = attn_fwd(False, tab, kv2, q2, *bias2, lo, oo)
    kv1, att2 = after(kv1, att2)
    att1, lse1 = attn_fwd(True, tab, kv1, q1, *bias1, lo, oo)
    halves2, halves1 = att2.reshape(2, rows, 128), att1.reshape(2, rows, 128)
    halves1, pair2, *far_w = after(halves1, swap(halves2[1], "cy"), *far_w, *pieces)
    far_w = far_w[:2] + [jnp.concatenate(far_w[2:])]
    att_rows = jnp.concatenate([halves2[0], halves1[0], pair2, swap(halves1[1], "cy")], axis=1)
    core_w = [swap(w, "fc") for w in own_w]
    last_w = [swap(w, "fc") for w in far_w]
    weights = list(zip(own_w, core_w, far_w, last_w))

    mid = up32(x) + dot_nt(w_o, att_rows)
    h2 = rms_cols(mid, gain_ffn).astype(BF)
    o_far = ffn_pair(h2, dy, *[w[2:] for w in weights])
    total = mid
    for r in (2, 3):
        total = total + dot_nn(weights[2][r], o_far[r - 2])
    fold = lambda o, k: up32(o[6 + k]) + up32(swap(o[9 + k], "fc"))
    far_g = [fold(o_far, k) for k in range(3)]
    cut = 2 * width // 3 // 16 * 16
    gate_far = far_g[0].astype(BF)
    to_x = [gate_far[:cut], gate_far[cut:], far_g[1].astype(BF)]
    keep_d, send_d = split_by(far_g[2], par)
    h2, total, keep_d, send_d, *to_x = after(h2, total, keep_d.astype(BF), send_d.astype(BF), *to_x)
    far_d = swap(send_d, "cy")
    gate_a, gate_b, far_up = [swap(g, "fx") for g in to_x]
    o_near = ffn_pair(h2, dy, *[w[:2] for w in weights])
    *o_near, far_d, gate_a = after(*o_near, far_d, gate_a)
    far_d = swap((up32(keep_d) + up32(far_d)).astype(BF), "fx")
    near_g = [fold(o_near, k) for k in range(3)]
    keep_d, send_d = split_by(near_g[2], par)
    near_d = swap(send_d.astype(BF), "cy")
    d_lists = [o_near[2], o_near[3], o_far[2], o_far[3], o_near[4], o_near[5], o_far[4], o_far[5]]
    w_lists = list(weights[0]) + list(weights[1])
    d_mid, d_branch, d_att, g_gain_ffn = ffn_back(d_lists, w_lists, mid, dy, gain_ffn, w_o)
    for r in (0, 1):
        total = total + dot_nn(weights[2][r], o_near[r])
    layer_out = jnp.transpose(total.astype(BF)).reshape(layer_in.shape)

    do1 = blocks(jnp.stack([d_att[:, 128:256], swap(d_att[:, 384:], "cy")]))
    do2 = blocks(jnp.stack([d_att[:, :128], swap(d_att[:, 256:384], "cy")]))
    do1, do2, far_d, near_d, far_gate = after(do1, do2, far_d, near_d, jnp.concatenate([gate_a, gate_b]))
    half_d = (keep_d + up32(near_d) + up32(far_d)).astype(BF)
    scatter = lambda v, dim: lax.psum_scatter(v, "cz", scatter_dimension=dim, tiled=True)
    piece_d = scatter(half_d, 0)
    keep_gate, send = split_by(near_g[0] + up32(far_gate), par)
    recv_gate = swap(send.astype(BF), "cy")
    dq1, dkv1, gt1, gz1 = attn_bwd(True, tab, kv1, q1, do1, att1, *bias1, lo, oo, lse1)
    dkv1, dq1, piece_d, recv_gate, far_up = after(dkv1, dq1, piece_d, recv_gate, far_up)
    dkv1 = scatter(dkv1.reshape(GROUP, 128), 0)
    half_gate = (keep_gate + up32(recv_gate)).astype(BF)
    piece_gate = scatter(half_gate, 0)
    keep_up, send = split_by(near_g[1] + up32(far_up), par)
    recv_up = swap(send.astype(BF), "cy")
    do2, far_up = after(do2, far_up)
    dq2, dkv2, gt2, gz2 = attn_bwd(False, tab, kv2, q2, do2, att2, *bias2, lo, oo, lse2)
    dkv2, dq2, dkv1, recv_up, piece_gate = after(dkv2, dq2, dkv1, recv_up, piece_gate)
    dkv2 = scatter(dkv2.reshape(GROUP, 256), 0)
    half_up = (keep_up + up32(recv_up)).astype(BF)
    g_out = dot_nn(d_branch, att_rows).astype(BF)
    dq1, dq2 = dq1.reshape(2, rows, 128), dq2.reshape(2, rows, 128)
    other1 = [swap(v, "cy") for v in (dkv1[rows:], dq1[1])]
    other_q2 = swap(dq2[1], "cy")
    dkv2, half_up, piece_d, piece_gate = after(dkv2, half_up, piece_d, piece_gate)
    other2 = [swap(dkv2[rows:], "cy"), other_q2]
    d_qkv = jnp.concatenate(
        [dkv2[:rows], dq2[0], dkv1[:rows], dq1[0]] + other2 + other1, axis=1)
    piece_up = scatter(half_up, 0)
    gather_half = lambda piece: lax.all_gather(piece, "cz", axis=0, tiled=True)

    def whole(half, other):
        return up32(jnp.concatenate([pick_half(par, half, other), pick_half(par, other, half)]))

    g_bias = bias_grads(gt2, gz2, gt1, gz1, table.shape[0])
    zero = jnp.zeros_like(g_bias)
    g_bias = jnp.concatenate([pick_half(par, g_bias, zero), pick_half(par, zero, g_bias)], axis=1)
    spare = jnp.pad(g_bias.reshape(shards, bias_rows, HEADS),
                    ((0, 0), (0, share - bias_rows), (66, 128 - 66 - HEADS))).reshape(width, 128)
    spare = jnp.where(jnp.arange(128)[None, :] == 65, g_gain_ffn, spare)
    in_grad, g_qkv = in_back(d_qkv, w_qkv, x, h1, gain_attn, d_mid, spare)
    in_grad = jnp.transpose(in_grad).reshape(layer_in.shape)

    f_here = lax.axis_index("fx") * 2 + lax.axis_index("fc")

    def fold_attn(g):
        blocks = g.reshape(shards, share, g.shape[1])
        away = lambda r: lax.dynamic_index_in_dim(blocks, f_here ^ r, keepdims=False)
        near = up32(away(0)) + up32(swap(away(1), "fc"))
        far = (up32(away(2)) + up32(swap(away(3), "fc"))).astype(BF)
        own = near + up32(swap(far, "fx"))
        half = g.shape[1] // 2
        own = pick_half(par, own, jnp.concatenate([own[:, half:], own[:, :half]], axis=1))
        return jnp.pad(own, ((0, (-share) % 64), (0, 0)))

    g_out = up32(ctx_gather(ctx_scatter(fold_attn(g_out), bits), bits)[:share])
    half_d = gather_half(piece_d)
    g_qkv, half_d, piece_up = after(g_qkv, half_d, piece_up)
    half_gate, half_up = gather_half(piece_gate), gather_half(piece_up)
    g_qkv, other_d = after(fold_attn(g_qkv), swap(half_d, "cy"))
    g_qkv, other_gate = after(ctx_scatter(g_qkv, bits), swap(half_gate, "cy"))
    g_qkv = up32(ctx_gather(g_qkv, bits)[:share])
    grad_down_t, grad_gate = whole(half_d, other_d), whole(half_gate, other_gate)
    grad_up = whole(half_up, swap(half_up, "cy"))
    cols = lambda g, at: g[:, at : at + HDIM]
    p0, p1 = 0, 640
    grad_key = jnp.concatenate([cols(g_qkv, p + o) for p in (p0, p1) for o in (0, 64, 384)], axis=1)
    grad_value = jnp.concatenate([cols(g_qkv, p + o) for p in (p0, p1) for o in (128, 192, 448)], axis=1)
    grad_query = jnp.concatenate([cols(g_qkv, p + o) for p in (p0, p1) for o in (256, 320, 512)], axis=1)
    grad_out = jnp.transpose(
        jnp.concatenate([cols(g_out, p + o) for p in (0, 256) for o in (0, 64, 192)], axis=1))
    rest = cols(g_qkv, 576) + cols(g_qkv, 1216)
    return (
        layer_out, in_grad, grad_query, grad_key, grad_value, grad_out, grad_gate, grad_up,
        jnp.transpose(grad_down_t), rest[:, 0], rest[:, 1], rest[:bias_rows, 2 : 2 + HEADS],
    )


def solution(mesh):
    devices = mesh.devices
    ctx_size, fsdp_size = mesh.shape["ctx"], mesh.shape["fsdp"]
    split = Mesh(devices.reshape(ctx_size // 2, 2, fsdp_size // 2, 2), ("cz", "cy", "fx", "fc"))
    cs, fs = ("cz", "cy"), ("fx", "fc")
    in_specs = (
        P(fs, cs, None), P(fs, cs, None), P(fs, None), P(fs, None), P(fs, None), P(None, fs),
        P(None, fs), P(None, fs), P(fs, None), P(fs), P(fs), P(fs, None), P(), P(fs, None),
    )
    out_specs = (
        P(fs, cs, None), P(fs, cs, None), P(fs, None), P(fs, None), P(fs, None), P(None, fs),
        P(None, fs), P(None, fs), P(fs, None), P(fs), P(fs), P(fs, None),
    )
    return jax.shard_map(
        on_device, mesh=split, in_specs=in_specs, out_specs=out_specs, check_vma=False
    )
```

```python
import functools
import math

import jax
import jax.numpy as jnp
from jax import lax
from jax.experimental import pallas as pl
from jax.experimental.pallas import tpu as pltpu
from jax.sharding import Mesh, PartitionSpec as P

HEADS = 6
HDIM = 64
PROMPT = 4096
NCONT = 8
BLK = 64
CONTS = 4096
GROUP = 8192
NBLK = GROUP // BLK
PBLK = PROMPT // BLK
LOG2E = 1.4426950408889634
NEG = -3e30
M_INIT = -1e30
WIN = 3
WK = WIN * BLK
FARB = 16
FK = FARB * BLK
thresholds = [math.ceil(16 * 8 ** (step_t / 16)) for step_t in range(1, 16)]
epsilon = 1e-06
BF = jnp.bfloat16
F32 = jnp.float32
HINT = 1 << 20


def dot_nt(a, b):
    return lax.dot_general(a, b, (((1,), (1,)), ((), ())), preferred_element_type=F32)


def dot_nn(a, b):
    return lax.dot_general(a, b, (((1,), (0,)), ((), ())), preferred_element_type=F32)


def dot_tn(a, b):
    return lax.dot_general(a, b, (((0,), (0,)), ((), ())), preferred_element_type=F32)


class Tab:
    def __init__(self, n):
        self.src = 0
        self.slot = NBLK
        self.blk = NBLK + n
        self.nch = NBLK + 2 * n
        self.zf = NBLK + 3 * n
        self.lim = NBLK + 4 * n
        self.size = NBLK + 5 * n


def lane(shape):
    return lax.broadcasted_iota(jnp.int32, shape, len(shape) - 1)


def sub(shape):
    return lax.broadcasted_iota(jnp.int32, shape, len(shape) - 2)


def stack_super(tab, t, src, dst, base, one, hi):
    low = lane((BLK, 128)) < 64
    for j in range(4):
        blk = src[tab[t.slot + base + j]]
        zero = jnp.zeros_like(blk)
        if one:
            dst[0, j * 64 : (j + 1) * 64, :] = jnp.where(low, zero, blk) if hi else jnp.where(low, blk, zero)
        else:
            u, r = j // 2, (j % 2) * 128
            dst[u, r : r + 64, :] = jnp.where(low, blk, zero)
            dst[u, r + 64 : r + 128, :] = jnp.where(low, zero, blk)


def near_parts(one):
    return [(0, 0), (0, 128)] if one else [(0, 0), (0, 128), (1, 0), (1, 128)]


def near_setup(base, one, z_ref, oo_ref, bias, oh):
    low = lane((WK, 128)) < 64
    for j in range(4):
        oh[j] = (sub((128, 128)) == oo_ref[base + j]).astype(BF)
    spread = lambda h, x: dot_nn(z_ref[0, h], x) + dot_nn(z_ref[1, h], x)
    if one:
        for p in range(2):
            bias[1, p] = spread(0, jnp.where(lane((128, 128)) < 64, oh[2 * p], oh[2 * p + 1]))
    else:
        for j in range(4):
            bias[1, j] = jnp.where(low, spread(0, oh[j]), spread(1, oh[j]))


def near_scalars(tab, t, base, i):
    offs, act = [], []
    for j in range(4):
        b = tab[t.blk + base + j]
        off = jnp.where(i == 0, b - (WIN - 1), jnp.where(i == 1, PBLK - WIN, b - (WIN - 1) - WIN * (i - 1)))
        active = i < tab[t.nch + base + j]
        offs.append(jnp.where(active, off, 0))
        act.append(active)
    return offs, act


def near_low(lo_ref, base, j, i, act):
    lo = lo_ref[base + j]
    lo = jnp.where(i == 1, jnp.zeros_like(lo), lo)
    return jnp.where(act[j], lo, jnp.full_like(lo, 1 << 20))


def near_keep(lo_ref, base, one, x, i, act, offs):
    edge = lambda j: near_low(lo_ref, base, j, i, act) - offs[j] * BLK
    if one:
        return sub((WK, 128)) >= jnp.where(lane((1, 128)) < 64, edge(2 * x), edge(2 * x + 1))
    return sub((WK, 128)) >= edge(x)


def near_dot(kv, wins, one, x, a, b, q):
    if one:
        left, right = [dot_nt(rows_of(kv, wins[2 * x + k], a, b), q) for k in range(2)]
        return jnp.where(lane(left.shape) < 64, left, right)
    return dot_nt(rows_of(kv, wins[x], a, b), q)


def near_dot_t(kv, wins, one, x, a, b, p):
    if one:
        left, right = [dot_tn(rows_of(kv, wins[2 * x + k], a, b), p) for k in range(2)]
        return jnp.where(lane(left.shape) < 64, left, right)
    return dot_tn(rows_of(kv, wins[x], a, b), p)


def near_scores(kv, qst, bias, lo_ref, base, one, i, offs, act, wins):
    kind = jnp.minimum(i, 2)
    out = []
    for x, (u, a) in enumerate(near_parts(one)):
        s = near_dot(kv, wins, one, x, 0, 128, qst[u, a : a + 128, :]) * LOG2E + bias[kind, x]
        out.append(jnp.where(near_keep(lo_ref, base, one, x, i, act, offs), s, NEG))
    return out


def far_mask(tab, t, base, one, u, c, shape):
    pos = c * FK + sub(shape)
    ln = lane(shape)
    lim = lambda j: tab[t.lim + base + j]
    if one:
        low = jnp.where(ln < 64, lim(0), lim(1))
        return pos < jnp.where(ln < 128, low, jnp.where(ln < 192, lim(2), lim(3)))
    return pos < jnp.where(ln < 128, lim(2 * u), lim(2 * u + 1))


def far_counts(tab, t, base):
    lims = [tab[t.lim + base + j] for j in range(4)]
    least = jnp.minimum(jnp.minimum(lims[0], lims[1]), jnp.minimum(lims[2], lims[3]))
    most = jnp.maximum(jnp.maximum(lims[0], lims[1]), jnp.maximum(lims[2], lims[3]))
    return least // FK, (most + FK - 1) // FK


def near_count(tab, t, base):
    ns = [tab[t.nch + base + j] for j in range(4)]
    return jnp.maximum(jnp.maximum(ns[0], ns[1]), jnp.maximum(ns[2], ns[3]))


def blocks_of(tab, t, first, count):
    return [tab[t.src + jnp.maximum(first + i, 0)] for i in range(count)]


def rows_of(ref, blocks, a, b):
    return jnp.concatenate([ref[i, :, a:b] for i in blocks], axis=0)


def transpose_far(tab, t, kv, dst, a, b):
    def step(c, carry):
        x = rows_of(kv, blocks_of(tab, t, c * FARB, FARB), a, b)
        dst[:, pl.ds(pl.multiple_of(c * FK, FK), FK)] = jnp.transpose(x)
        return carry

    lax.fori_loop(0, PROMPT // FK, step, 0)


def start_bias(t_ref, bias):
    for x in range(bias.shape[1]):
        bias[0, x] = t_ref[...]
        bias[2, x] = jnp.zeros((WK, 128), F32)


def give_rows(tab, t, base, one, u, val, dst, hi):
    low = lane((BLK, 128)) < 64
    if one:
        for j in range(4):
            piece = val[j * 64 : (j + 1) * 64]
            zero = jnp.zeros_like(piece)
            dst[tab[t.slot + base + j]] = (jnp.where(low, zero, piece) if hi else jnp.where(low, piece, zero)).astype(BF)
    else:
        for k in range(2):
            r = k * 128
            dst[tab[t.slot + base + 2 * u + k]] = jnp.where(low, val[r : r + 64], val[r + 64 : r + 128]).astype(BF)


def fwd_kernel(n, one, tab, kv, qs, t_ref, z_ref, lo_ref, oo_ref, o_ref, lse_ref, qst, vt, bias, oh, m, l, acc):
    t = Tab(n)
    units = 1 if one else 2
    va, vb = (0, 128) if one else (128, 256)
    transpose_far(tab, t, kv, vt, va, vb)
    start_bias(t_ref, bias)

    def update(at, ss, pv):
        olds = [m[u, :, a:b] for u, a, b in at]
        news = [jnp.maximum(old, jnp.max(s, axis=0, keepdims=True)) for old, s in zip(olds, ss)]
        ps = [jnp.exp2(s - new) for s, new in zip(ss, news)]
        al = [jnp.exp2(old - new) for old, new in zip(olds, news)]
        sums = [jnp.sum(p, axis=0, keepdims=True) for p in ps]
        outs = [pv(x, p.astype(BF)) for x, p in enumerate(ps)]
        for x, (u, a, b) in enumerate(at):
            m[u, :, a:b] = news[x]
            l[u, :, a:b] = l[u, :, a:b] * al[x] + sums[x]
            acc[u, :, a:b] = acc[u, :, a:b] * al[x] + outs[x]

    def super_tile(s_i, carry):
        base = s_i * 4
        stack_super(tab, t, qs, qst, base, one, False)
        m[...] = jnp.full(m.shape, M_INIT, F32)
        l[...] = jnp.zeros(l.shape, F32)
        acc[...] = jnp.zeros(acc.shape, F32)
        n_near = near_count(tab, t, base)

        @pl.when(n_near > 1)
        def _():
            near_setup(base, one, z_ref, oo_ref, bias, oh)

        def near(i, carry):
            offs, act = near_scalars(tab, t, base, i)
            wins = [blocks_of(tab, t, off, WIN) for off in offs]
            ss = near_scores(kv, qst, bias, lo_ref, base, one, i, offs, act, wins)
            at = [(u, a, a + 128) for u, a in near_parts(one)]
            update(at, ss, lambda x, p: near_dot_t(kv, wins, one, x, va, vb, p))
            return carry

        lax.fori_loop(0, n_near, near, 0)

        def far(masked, c, carry):
            k = rows_of(kv, blocks_of(tab, t, c * FARB, FARB), 0, 128)
            ss = [dot_nt(k, qst[u]) * LOG2E for u in range(units)]
            if masked:
                ss = [jnp.where(far_mask(tab, t, base, one, u, c, s.shape), s, NEG) for u, s in enumerate(ss)]
            v = vt[:, pl.ds(pl.multiple_of(c * FK, FK), FK)]
            update([(u, 0, 256) for u in range(units)], ss, lambda x, p: dot_nn(v, p))
            return carry

        n_full, n_far = far_counts(tab, t, base)
        lax.fori_loop(0, n_full, functools.partial(far, False), 0)
        lax.fori_loop(n_full, n_far, functools.partial(far, True), 0)
        for u in range(units):
            lse_ref[s_i, u] = m[u] + jnp.log(l[u]) * LOG2E
            give_rows(tab, t, base, one, u, jnp.transpose(acc[u] / l[u]), o_ref, True)
        return carry

    lax.fori_loop(0, n // 4, super_tile, 0)


def bwd_kernel(n, one, tab, kv, qs, dos, ats, t_ref, z_ref, lo_ref, oo_ref, lse_ref,
               dq_ref, dkv_ref, gt_ref, gz_ref, dkv, qst, dst, qm, dm, kt, bias, oh, gn, dq, delta):
    t = Tab(n)
    units = 1 if one else 2
    va, vb = (0, 128) if one else (128, 256)
    parts = near_parts(one)
    transpose_far(tab, t, kv, kt, 0, 128)
    start_bias(t_ref, bias)

    def clear(p, carry):
        dkv[p] = jnp.zeros(dkv.shape[1:], F32)
        return carry

    lax.fori_loop(0, NBLK, clear, 0)
    gn[...] = jnp.zeros(gn.shape, F32)
    gz_ref[...] = jnp.zeros(gz_ref.shape, F32)

    def add_rows(blocks, a, b, val):
        for i, block in enumerate(blocks):
            dkv[block, :, a:b] += val[i * BLK : (i + 1) * BLK]

    def super_tile(s_i, carry):
        base = s_i * 4
        stack_super(tab, t, qs, qst, base, one, False)
        stack_super(tab, t, dos, dst, base, one, True)
        if one:
            half_rows = sub((128, 128)) < 64
            for x in range(2):
                for src, dst_m in ((qst, qm), (dst, dm)):
                    val = src[0, x * 128 : (x + 1) * 128, :]
                    zero = jnp.zeros_like(val)
                    dst_m[x, 0] = jnp.where(half_rows, val, zero)
                    dst_m[x, 1] = jnp.where(half_rows, zero, val)
        low = lane((BLK, 128)) < 64
        zero = jnp.zeros((BLK, 128), F32)
        prods = []
        for j in range(4):
            slot = tab[t.slot + base + j]
            prods.append(dos[slot].astype(F32) * ats[slot].astype(F32))
        for u in range(units):
            if one:
                stacked = [jnp.where(low, zero, p) for p in prods]
            else:
                stacked = [x for p in prods[2 * u : 2 * u + 2] for x in (jnp.where(low, p, zero), jnp.where(low, zero, p))]
            delta[u] = jnp.sum(jnp.transpose(jnp.concatenate(stacked, axis=0)), axis=0, keepdims=True)
        dq[...] = jnp.zeros(dq.shape, F32)
        n_near = near_count(tab, t, base)

        @pl.when(n_near > 1)
        def _():
            near_setup(base, one, z_ref, oo_ref, bias, oh)

        def near(i, carry):
            offs, act = near_scalars(tab, t, base, i)
            wins = [blocks_of(tab, t, off, WIN) for off in offs]
            ss = near_scores(kv, qst, bias, lo_ref, base, one, i, offs, act, wins)
            dps = [near_dot(kv, wins, one, x, va, vb, dst[u, a : a + 128, :]) for x, (u, a) in enumerate(parts)]
            ps = [jnp.exp2(s - lse_ref[s_i, u, :, a : a + 128]) for s, (u, a) in zip(ss, parts)]
            ds = [(p * (dp - delta[u, :, a : a + 128])).astype(BF) for p, dp, (u, a) in zip(ps, dps, parts)]
            pb = [p.astype(BF) for p in ps]
            dqs = [near_dot_t(kv, wins, one, x, 0, 128, ds[x]) for x in range(len(parts))]
            adds = []
            for x, (u, a) in enumerate(parts):
                if one:
                    for k in range(2):
                        adds.append((wins[2 * x + k], 0, 128, dot_nn(ds[x], qm[x, k]) + dot_nn(pb[x], dm[x, k])))
                else:
                    adds.append((wins[x], 0, 128, dot_nn(ds[x], qst[u, a : a + 128, :])))
                    adds.append((wins[x], va, vb, dot_nn(pb[x], dst[u, a : a + 128, :])))
            for add in adds:
                add_rows(*add)
            for x, (u, a) in enumerate(parts):
                slot = jnp.where(i == 0, 0, jnp.where(i == 1, 1 + x, 1 + len(parts)))
                gn[slot] += ds[x].astype(F32)
                dq[u, :, a : a + 128] += dqs[x]
            return carry

        lax.fori_loop(0, n_near, near, 0)

        @pl.when(n_near > 1)
        def _():
            half = lane((128, 128)) < 64
            none = jnp.zeros((128, 128), BF)
            for x in range(len(parts)):
                g = gn[1 + x].astype(BF)
                if one:
                    gz_ref[0] += dot_nt(g, jnp.where(half, oh[2 * x], oh[2 * x + 1]))
                else:
                    gz_ref[0] += dot_nt(g, jnp.where(half, oh[x], none))
                    gz_ref[1] += dot_nt(g, jnp.where(half, none, oh[x]))
                gn[1 + x] = jnp.zeros((WK, 128), F32)

        def far(masked, c, carry):
            blocks = blocks_of(tab, t, c * FARB, FARB)
            k = rows_of(kv, blocks, 0, 128)
            v = k if one else rows_of(kv, blocks, va, vb)
            ss = [dot_nt(k, qst[u]) * LOG2E for u in range(units)]
            dps = [dot_nt(v, dst[u]) for u in range(units)]
            if masked:
                ss = [jnp.where(far_mask(tab, t, base, one, u, c, s.shape), s, NEG) for u, s in enumerate(ss)]
            ps = [jnp.exp2(s - lse_ref[s_i, u]) for u, s in enumerate(ss)]
            ds = [(p * (dp - delta[u])).astype(BF) for u, (p, dp) in enumerate(zip(ps, dps))]
            pb = [p.astype(BF) for p in ps]
            if one:
                add_rows(blocks, 0, 128, dot_nn(ds[0], qst[0]) + dot_nn(pb[0], dst[0]))
            else:
                add_rows(blocks, 0, 128, dot_nn(ds[0], qst[0]) + dot_nn(ds[1], qst[1]))
                add_rows(blocks, va, vb, dot_nn(pb[0], dst[0]) + dot_nn(pb[1], dst[1]))
            for u in range(units):
                dq[u] += dot_nn(kt[:, pl.ds(pl.multiple_of(c * FK, FK), FK)], ds[u])
            return carry

        n_full, n_far = far_counts(tab, t, base)
        lax.fori_loop(0, n_full, functools.partial(far, False), 0)
        lax.fori_loop(n_full, n_far, functools.partial(far, True), 0)
        for u in range(units):
            give_rows(tab, t, base, one, u, jnp.transpose(dq[u]), dq_ref, False)
        return carry

    lax.fori_loop(0, n // 4, super_tile, 0)
    gt_ref[...] = gn[0]

    def give(p, carry):
        dkv_ref[p] = dkv[p].astype(BF)
        return carry

    lax.fori_loop(0, NBLK, give, 0)


VM = pl.BlockSpec(memory_space=pltpu.VMEM)
HB = pl.BlockSpec(memory_space=pl.ANY)
SM = pl.BlockSpec(memory_space=pltpu.SMEM)


def attn_fwd(one, tab, kv, q, t_tab, z_tab, lo, oo):
    n = q.shape[0]
    units, parts = (1, 2) if one else (2, 4)
    return pl.pallas_call(
        functools.partial(fwd_kernel, n, one),
        out_shape=(
            jax.ShapeDtypeStruct((n, BLK, 128), BF),
            jax.ShapeDtypeStruct((n // 4, units, 1, 256), F32),
        ),
        in_specs=[SM] + [VM] * 6,
        out_specs=(VM, VM),
        scratch_shapes=[
            pltpu.VMEM((units, 256, 128), BF),
            pltpu.VMEM((128, PROMPT), BF),
            pltpu.VMEM((3, parts, WK, 128), F32),
            pltpu.VMEM((4, 128, 128), BF),
            pltpu.VMEM((units, 1, 256), F32),
            pltpu.VMEM((units, 1, 256), F32),
            pltpu.VMEM((units, 128, 256), F32),
        ],
        compiler_params=pltpu.CompilerParams(vmem_limit_bytes=30 << 20),
        cost_estimate=pl.CostEstimate(flops=HINT, bytes_accessed=HINT, transcendentals=0),
        name="attn_fwd_one" if one else "attn_fwd_two",
    )(tab, kv, q, t_tab, z_tab, lo, oo)


def attn_bwd(one, tab, kv, q, do, at, t_tab, z_tab, lo, oo, lse):
    n = q.shape[0]
    units, parts = (1, 2) if one else (2, 4)
    lanes = kv.shape[2]
    masked = (2, 2, 128, 128) if one else (1, 1, 16, 128)
    return pl.pallas_call(
        functools.partial(bwd_kernel, n, one),
        out_shape=(
            jax.ShapeDtypeStruct((n, BLK, 128), BF),
            jax.ShapeDtypeStruct((NBLK, BLK, lanes), BF),
            jax.ShapeDtypeStruct((WK, 128), F32),
            jax.ShapeDtypeStruct((units, WK, 128), F32),
        ),
        in_specs=[SM] + [VM] * 9,
        out_specs=(VM, VM, VM, VM),
        scratch_shapes=[
            pltpu.VMEM((NBLK, BLK, lanes), F32),
            pltpu.VMEM((units, 256, 128), BF),
            pltpu.VMEM((units, 256, 128), BF),
            pltpu.VMEM(masked, BF),
            pltpu.VMEM(masked, BF),
            pltpu.VMEM((128, PROMPT), BF),
            pltpu.VMEM((3, parts, WK, 128), F32),
            pltpu.VMEM((4, 128, 128), BF),
            pltpu.VMEM((2 + parts, WK, 128), F32),
            pltpu.VMEM((units, 128, 256), F32),
            pltpu.VMEM((units, 1, 256), F32),
        ],
        compiler_params=pltpu.CompilerParams(vmem_limit_bytes=44 << 20),
        cost_estimate=pl.CostEstimate(flops=HINT, bytes_accessed=HINT, transcendentals=0),
        name="attn_bwd_one" if one else "attn_bwd_two",
    )(tab, kv, q, do, at, t_tab, z_tab, lo, oo, lse)


def bucket_of(distance):
    distance = jnp.maximum(distance, 0)
    far_bucket = jnp.full(distance.shape, 16, jnp.int32)
    for threshold in thresholds:
        far_bucket = far_bucket + (distance >= threshold).astype(jnp.int32)
    return jnp.where(distance < 16, distance, far_bucket)


def near_distance():
    diag = (WIN - 1) * BLK + jnp.arange(BLK)[None, :] - jnp.arange(WK)[:, None]
    tail = WK + jnp.arange(128)[None, :] - jnp.arange(WK)[:, None]
    return diag.astype(jnp.int32), tail.astype(jnp.int32)


def bucket_in(distance, low, high):
    bucket = jnp.minimum(jnp.maximum(distance, 0), 16)
    for threshold in thresholds:
        if threshold <= high:
            bucket = bucket + (distance >= threshold).astype(jnp.int32)
    return bucket


def tables_kernel(last, table, two, z_two, one, z_one):
    diag = (WIN - 1) * BLK + lane((WK, 128)) % 64 - sub((WK, 128))
    tail = WK + lane((WK, 128)) - sub((WK, 128))
    left = lane((WK, 128)) < 64
    near, end = bucket_in(diag, -WK, WK), bucket_in(tail, 1, WK + 128)
    rel = lambda b, h: (table[b * 3 + h] - table[last * 3 + h]) * LOG2E
    zero = jnp.zeros((WK, 128), F32)
    picks = [zero] * 6
    for b in range(last):
        at_near, at_end = near == b, end == b
        picks = [jnp.where(at_near, rel(b, h), picks[h]) for h in range(3)] + [
            jnp.where(at_end, rel(b, h), picks[3 + h]) for h in range(3)]
    seen = diag >= 0
    two[...] = jnp.where(seen, jnp.where(left, picks[0], picks[1]), NEG)
    one[...] = jnp.where(seen, picks[2], NEG)
    for ref, i, val in ((z_two, 0, picks[3]), (z_two, 1, picks[4]), (z_one, 0, picks[5])):
        high = val.astype(BF)
        ref[0, i] = high
        ref[1, i] = (val - high.astype(F32)).astype(BF)


def bias_tables(table):
    shape = jax.ShapeDtypeStruct
    two, z_two, one, z_one = pl.pallas_call(
        functools.partial(tables_kernel, table.shape[0] - 1),
        out_shape=(shape((WK, 128), F32), shape((2, 2, WK, 128), BF), shape((WK, 128), F32), shape((2, 1, WK, 128), BF)),
        in_specs=[SM],
        out_specs=(VM, VM, VM, VM),
        cost_estimate=pl.CostEstimate(flops=HINT, bytes_accessed=HINT, transcendentals=0),
        name="tables",
    )(table.reshape(-1))
    return (two, z_two), (one, z_one)


def bias_grads(gt_two, gz_two, gt_one, gz_one, buckets):
    diag, tail = near_distance()
    gd = jnp.stack([gt_two[:, :64], gt_two[:, 64:], gt_one[:, :64] + gt_one[:, 64:]])
    gz = jnp.concatenate([gz_two, gz_one])
    bd, bt = bucket_of(diag), bucket_of(tail)
    labels = jnp.arange(buckets - 1, dtype=jnp.int32)[:, None, None, None]
    seen = diag >= 0
    one = jnp.sum(jnp.where((bd[None, None] == labels) & seen[None, None], gd[None], 0.0), axis=(2, 3))
    two = jnp.sum(jnp.where(bt[None, None] == labels, gz[None], 0.0), axis=(2, 3))
    near = one + two
    return jnp.concatenate([near, -jnp.sum(near, axis=0, keepdims=True)], axis=0)


def plan(deal_table, seg_row, ctx, nb):
    n = 2 * nb
    par = ctx % 2
    slot = jnp.arange(NBLK, dtype=jnp.int32)
    owner = slot // nb
    where_kv = ((owner // 2) * 2 + (owner % 2 + par) % 2) * nb + slot % nb
    src = jnp.sum(jnp.where(deal_table[None, :] == slot[:, None], where_kv[None, :], 0), axis=1)
    own = lax.dynamic_slice_in_dim(deal_table, ctx * nb, nb)
    other = lax.dynamic_slice_in_dim(deal_table, (ctx + 1 - 2 * par) * nb, nb)
    rb = jnp.concatenate([own, other])
    rank = jnp.sum((rb[None, :] < rb[:, None]).astype(jnp.int32), axis=1)
    pos = jnp.arange(n, dtype=jnp.int32)
    pick = (rank[None, :] == pos[:, None]).astype(jnp.int32)
    rslot = jnp.sum(pick * pos[None, :], axis=1)
    rblk = jnp.sum(pick * rb[None, :], axis=1)
    labels = jnp.arange(NCONT, dtype=jnp.int32)
    starts = jnp.sum((seg_row[None, :] < labels[:, None]).astype(jnp.int32), axis=1)
    cpos = rblk[:, None] * BLK + jnp.arange(BLK, dtype=jnp.int32)[None, :] - PROMPT
    ss = jnp.max(jnp.where(starts[None, None, :] <= cpos[:, :, None], starts[None, None, :], 0), axis=2)
    is_cont = rblk >= PBLK
    lo = jnp.where(is_cont[:, None], PROMPT + ss, 0)
    oo = jnp.where(is_cont[:, None], jnp.minimum(cpos - ss, 127), 127)
    first = (PROMPT + ss[:, 0]) // BLK
    more = jnp.maximum(rblk - (WIN - 1) - first, 0)
    nch = jnp.where(is_cont, 2 + (more + WIN - 1) // WIN, 1)
    zf = jnp.zeros_like(nch)
    lim = jnp.where(is_cont, PROMPT - WK, jnp.maximum(rblk - (WIN - 1), 0) * BLK)
    tab = jnp.concatenate([src, rslot, rblk, nch, zf, lim]).astype(jnp.int32)
    dup = lambda x: jnp.concatenate([x, x], axis=1)[:, None, :].astype(jnp.int32)
    return tab, dup(lo), dup(oo)


def gelu_parts(v):
    c = math.sqrt(2 / math.pi)
    sq = v * v
    th = jnp.tanh(c * v * (1 + 0.044715 * sq))
    half = 0.5 * (1 + th)
    return v * half, half + 0.5 * c * v * (1 - th * th) * (1 + 3 * 0.044715 * sq)


def ffn_kernel(h, dy, wga, wgb, wua, wub, wda, wdb, hida, hidb, dga, dgb, dua, dub, *g_refs):
    rows = h.shape[1]
    step = min(256, rows)
    w_in = jnp.transpose(jnp.concatenate([wga[...], wgb[...], wua[...], wub[...]], axis=1))
    w_down = jnp.transpose(jnp.concatenate([wda[...], wdb[...]], axis=1))
    for r in range(0, rows, step):
        both = dot_nn(w_in, h[:, r : r + step])
        d_hidden = dot_nn(w_down, dy[:, r : r + step])
        gate, up = both[:256], both[256:]
        act, slope = gelu_parts(gate)
        for a, b, val in ((hida, hidb, act * up), (dga, dgb, d_hidden * up * slope), (dua, dub, d_hidden * act)):
            val = val.astype(BF)
            a[:, r : r + step] = val[:128]
            b[:, r : r + step] = val[128:]
    for k, (left, a, b) in enumerate(((h, dga, dgb), (h, dua, dub), (dy, hida, hidb))):
        g = dot_nt(left[...], jnp.concatenate([a[...], b[...]], axis=0)).astype(BF)
        g_refs[k][...] = g[:, :128]
        g_refs[k + 3][...] = g[:, 128:]


def ffn_pair(h, dy, gates, ups, downs):
    width, rows = h.shape
    units = gates[0].shape[1]
    whole = pl.BlockSpec((width, rows), lambda i: (0, 0), pipeline_mode=pl.Buffered(1))
    col = pl.BlockSpec((width, 128), lambda i: (0, i))
    act = pl.BlockSpec((128, rows), lambda i: (i, 0))
    return pl.pallas_call(
        ffn_kernel,
        grid=(units // 128,),
        out_shape=[jax.ShapeDtypeStruct((units, rows), BF)] * 6 + [jax.ShapeDtypeStruct((width, units), BF)] * 6,
        in_specs=[whole, whole] + [col] * 6,
        out_specs=[act] * 6 + [col] * 6,
        compiler_params=pltpu.CompilerParams(vmem_limit_bytes=44 << 20),
        cost_estimate=pl.CostEstimate(flops=HINT, bytes_accessed=HINT, transcendentals=0),
        name="ffn_pair",
    )(h, dy, *gates, *ups, *downs)


def each(count, body):
    def step(i, carry):
        body(i)
        return carry

    lax.fori_loop(0, count, step, 0)


def norm_back(x_at, d_at, gain, g_gain, rows, give):
    width = gain.shape[0]
    part = width // 8
    feats = [slice(f * part, (f + 1) * part) for f in range(8)]
    cols = min(256, rows)
    g_gain[...] = jnp.zeros(g_gain.shape, F32)

    def body(i):
        at = pl.ds(pl.multiple_of(i * cols, cols), cols)
        sq = jnp.zeros((1, cols), F32)
        dot = jnp.zeros((1, cols), F32)
        for f in feats:
            x = x_at[f, at].astype(F32)
            sq = sq + jnp.sum(x * x, axis=0, keepdims=True)
            dot = dot + jnp.sum(d_at[f, at] * gain[f, :] * x, axis=0, keepdims=True)
        rs = lax.rsqrt(sq / width + epsilon)
        coef = rs * rs * rs * dot / width
        for f in feats:
            x, d = x_at[f, at].astype(F32), d_at[f, at]
            give(f, at, rs * (d * gain[f, :]) - x * coef)
            g_gain[f, :] += jnp.sum(d * (x * rs), axis=1, keepdims=True)

    each(rows // cols, body)


def ffn_back_kernel(*refs):
    ds, ws = refs[:8], refs[8:16]
    mid_in, dy_in, gain, w_o_in, d_mid, d_branch, d_att, g_gain, dbuf, wbuf, mid, dy, w_o, acc, sems, late = refs[16:]
    slots = dbuf.shape[0]
    shards = len(ds) // 2

    def copies(i):
        s = i % slots
        return [pltpu.make_async_copy(src[i + k * shards], dst.at[s, k], sems.at[s, w, k])
                for k in range(2) for w, (src, dst) in enumerate(((ds, dbuf), (ws, wbuf)))]

    others = [pltpu.make_async_copy(a, b, late.at[i])
              for i, (a, b) in enumerate(((mid_in, mid), (dy_in, dy), (w_o_in, w_o)))]
    for i in range(slots):
        for c in copies(i):
            c.start()
    for c in others:
        c.start()
    rows = mid.shape[1]
    cols = min(512, rows)

    def add(i, s):
        def body(c):
            at = pl.ds(pl.multiple_of(c * cols, cols), cols)
            part = dot_nn(
                jnp.concatenate([wbuf[s, 0], wbuf[s, 1]], axis=1),
                jnp.concatenate([dbuf[s, 0, :, at], dbuf[s, 1, :, at]], axis=0),
            )
            if i == 0:
                acc[:, at] = part
            else:
                acc[:, at] += part

        each(rows // cols, body)

    for i in range(shards):
        s = i % slots
        for c in copies(i):
            c.wait()
        add(i, s)
        if i + slots < shards:
            for c in copies(i + slots):
                c.start()
    for c in others:
        c.wait()

    def give(f, at, val):
        val = dy[f, at].astype(F32) + val
        d_mid[f, at] = val
        d_branch[f, at] = val.astype(BF)

    norm_back(mid, acc, gain, g_gain, rows, give)

    def out(c):
        at = pl.ds(pl.multiple_of(c * cols, cols), cols)
        d_att[at, :] = dot_tn(d_branch[:, at], w_o[...]).astype(BF)

    each(rows // cols, out)


def ffn_back(d_list, w_list, mid, dy, gain, w_o):
    width, rows = mid.shape
    units = d_list[0].shape[0]
    return pl.pallas_call(
        ffn_back_kernel,
        out_shape=(
            jax.ShapeDtypeStruct((width, rows), F32),
            jax.ShapeDtypeStruct((width, rows), BF),
            jax.ShapeDtypeStruct((rows, w_o.shape[1]), BF),
            jax.ShapeDtypeStruct((width, 1), F32),
        ),
        in_specs=[HB] * 18 + [VM, HB],
        out_specs=(VM, VM, VM, VM),
        scratch_shapes=[
            pltpu.VMEM((2, 2, units, rows), BF),
            pltpu.VMEM((2, 2, width, units), BF),
            pltpu.VMEM((width, rows), F32),
            pltpu.VMEM((width, rows), BF),
            pltpu.VMEM(w_o.shape, BF),
            pltpu.VMEM((width, rows), F32),
            pltpu.SemaphoreType.DMA((2, 2, 2)),
            pltpu.SemaphoreType.DMA((3,)),
        ],
        compiler_params=pltpu.CompilerParams(vmem_limit_bytes=58 << 20),
        cost_estimate=pl.CostEstimate(flops=HINT, bytes_accessed=HINT, transcendentals=0),
        name="ffn_back",
    )(*d_list, *w_list, mid, dy, gain, w_o)


def in_part_kernel(d_qkv, w_qkv, h, part, g_qkv):
    rows = h.shape[1]
    cols = min(256, rows)

    def grads(c):
        at = pl.ds(pl.multiple_of(c * 256, 256), 256)
        g_qkv[:, at] = dot_nn(h[...], d_qkv[:, at]).astype(BF)

    each(d_qkv.shape[1] // 256, grads)

    def back(c):
        at = pl.ds(pl.multiple_of(c * cols, cols), cols)
        part[:, at] = dot_nt(w_qkv[...], d_qkv[at, :])

    each(rows // cols, back)


def in_part(d_qkv, w_qkv, h):
    width, rows = h.shape
    return pl.pallas_call(
        in_part_kernel,
        out_shape=(
            jax.ShapeDtypeStruct((width, rows), F32),
            jax.ShapeDtypeStruct((width, d_qkv.shape[1]), BF),
        ),
        in_specs=[VM] * 3,
        out_specs=(VM, VM),
        compiler_params=pltpu.CompilerParams(vmem_limit_bytes=40 << 20),
        cost_estimate=pl.CostEstimate(flops=HINT, bytes_accessed=HINT, transcendentals=0),
        name="in_part",
    )(d_qkv, w_qkv, h)


def in_back_kernel(d_qkv, w_qkv, part, x, h, gain, d_mid, extra, in_grad, g_qkv, acc, g_gain):
    width, rows = x.shape
    cols = min(256, rows)
    count = d_qkv.shape[1]

    def grads(c):
        at = pl.ds(pl.multiple_of(c * 256, 256), 256)
        g_qkv[:, at] = dot_nn(h[...], d_qkv[:, at]).astype(BF)

    each(count // 256, grads)

    def back(c):
        at = pl.ds(pl.multiple_of(c * cols, cols), cols)
        acc[:, at] = part[:, at] + dot_nt(w_qkv[...], d_qkv[at, :])

    each(rows // cols, back)

    def give(f, at, val):
        in_grad[f, at] = (d_mid[f, at] + val).astype(BF)

    norm_back(x, acc, gain, g_gain, rows, give)
    ln = lane((width, 128))
    g_qkv[:, count : count + 128] = jnp.where(ln == 0, g_gain[...], extra[...]).astype(BF)


def in_back(d_qkv, w_qkv, part, x, h, gain, d_mid, extra):
    width, rows = x.shape
    return pl.pallas_call(
        in_back_kernel,
        out_shape=(
            jax.ShapeDtypeStruct((width, rows), BF),
            jax.ShapeDtypeStruct((width, d_qkv.shape[1] + 128), BF),
        ),
        in_specs=[VM] * 8,
        out_specs=(VM, VM),
        scratch_shapes=[pltpu.VMEM((width, rows), F32), pltpu.VMEM((width, 1), F32)],
        compiler_params=pltpu.CompilerParams(vmem_limit_bytes=56 << 20),
        cost_estimate=pl.CostEstimate(flops=HINT, bytes_accessed=HINT, transcendentals=0),
        name="in_back",
    )(d_qkv, w_qkv, part, x, h, gain, d_mid, extra)


def pack_kernel(par, w_q, w_k, w_v, w_o, norms, table, qkv_out, o_out):
    low = lane((w_q.shape[0], 128)) < 64
    even = par[0] == 0
    tiles = lambda w: [w[:, i : i + 128].astype(F32) for i in (0, 128, 256)]
    turn = lambda v: pltpu.roll(v, 64, 1)

    def heads(w):
        a, b, c = tiles(w)
        return (a, b, turn(b)), (jnp.where(low, turn(b), turn(c)), turn(c), c)

    def packs(w):
        one, two = heads(w)
        choose = lambda x, y: jnp.where(even, x, y)
        return [tuple(choose(x, y) for x, y in zip(one, two)), tuple(choose(y, x) for x, y in zip(one, two))]

    spare = dot_tn(norms[...], (lane((8, 128)) == sub((8, 128)) + 64).astype(BF))
    pad = jnp.zeros((w_q.shape[0] - table.shape[0], 128), F32)
    spare = spare + jnp.concatenate([table[...], pad], axis=0)
    q, k, v, o = packs(w_q), packs(w_k), packs(w_v), packs(w_o)
    for p in range(2):
        third = jnp.where(low, q[p][1], spare if p == 0 else jnp.zeros_like(spare))
        for i, val in enumerate((k[p][0], v[p][0], q[p][0], jnp.where(low, k[p][1], v[p][2]), third)):
            qkv_out[:, p * 640 + i * 128 : p * 640 + (i + 1) * 128] = val.astype(BF)
        o_out[:, p * 256 : p * 256 + 128] = o[p][0].astype(BF)
        o_out[:, p * 256 + 128 : (p + 1) * 256] = jnp.where(low, jnp.zeros_like(spare), o[p][2]).astype(BF)


def pack(par, w_q, w_k, w_v, w_o, norm_attn, norm_ffn, rel_bias):
    share = w_q.shape[0]
    norms = jnp.pad(jnp.stack([norm_attn, norm_ffn]), ((0, 6), (0, 0)))
    rows = rel_bias.shape[0]
    table = jnp.pad(rel_bias.astype(F32), ((0, (-rows) % 8), (66, 128 - 66 - rel_bias.shape[1])))
    return pl.pallas_call(
        pack_kernel,
        out_shape=(jax.ShapeDtypeStruct((share, 1280), BF), jax.ShapeDtypeStruct((share, 512), BF)),
        in_specs=[SM] + [VM] * 6,
        out_specs=(VM, VM),
        cost_estimate=pl.CostEstimate(flops=HINT, bytes_accessed=HINT, transcendentals=0),
        name="pack",
    )(par.reshape(1), w_q, w_k, w_v, w_o, norms, table)


def swap(x, axis):
    return lax.ppermute(x, axis, [(0, 1), (1, 0)])


def pick_half(par, even, odd):
    return jnp.where(par == 0, even, odd)


def up32(x):
    return x.astype(F32)


def rms_cols(x, gain):
    return x * lax.rsqrt(jnp.mean(x * x, axis=0, keepdims=True) + epsilon) * gain


def after(*values):
    return lax.optimization_barrier(values)


def ctx_bits(cz, par, steps):
    out = [(par, lambda x: swap(x, "cy"))]
    bit = 1
    while bit < steps:
        perm = [(i, i ^ bit) for i in range(steps)]
        out.append(((cz // bit) % 2, lambda x, perm=perm: lax.ppermute(x, "cz", perm)))
        bit *= 2
    return out


def split_by(v, bit):
    half = v.shape[0] // 2
    return pick_half(bit, v[:half], v[half:]), pick_half(bit, v[half:], v[:half])


def ctx_scatter(v, bits):
    for bit, move in bits:
        keep, send = split_by(v, bit)
        v = up32(keep) + up32(move(send.astype(BF)))
    return v.astype(BF)


def ctx_gather(v, bits):
    for bit, move in reversed(bits):
        other = move(v)
        v = jnp.concatenate([pick_half(bit, v, other), pick_half(bit, other, v)])
    return v


def on_device(
    layer_in, out_grad, w_query, w_key, w_value, w_out, w_gate, w_up, w_down,
    norm_attn, norm_ffn, rel_bias, deal_table, seg_ids,
):
    _, rows, width = layer_in.shape
    nb = rows // BLK
    cz, par = lax.axis_index("cz"), lax.axis_index("cy")
    steps = lax.axis_size("cz")
    ctx = cz * 2 + par
    share = w_query.shape[0]
    fs = ("fx", "fc")
    shards = width // share
    bits = ctx_bits(cz, par, steps)

    w_qkv, w_o = pack(par, w_query, w_key, w_value, jnp.transpose(w_out), norm_attn, norm_ffn, rel_bias)
    w_qkv = lax.all_gather(w_qkv, fs, axis=0, tiled=True)
    gain_attn = up32(w_qkv[:, 576:577])
    gain_ffn = up32(w_qkv[:, 577:578])
    bias_rows = rel_bias.shape[0]
    table = w_qkv.reshape(shards, share, 1280)[:, :bias_rows, 578 : 578 + HEADS]
    table = up32(table.reshape(shards * bias_rows, HEADS))
    my_table = pick_half(par, table[:, :3], table[:, 3:])

    own_w = (w_gate, w_up, jnp.transpose(w_down))
    w_qkv, w_o, *sent = after(w_qkv, w_o, *own_w)
    w_o = lax.all_gather(w_o, fs, axis=0, tiled=True)
    quarter = width // 4
    pieces = [swap(sent[2][i * quarter : j * quarter], "fx") for i, j in ((0, 1), (1, 2), (2, 4))]
    far_w = [swap(w, "fx") for w in sent[:2]]

    x = jnp.transpose(layer_in.reshape(rows, width))
    dy = jnp.transpose(out_grad.reshape(rows, width))
    h1 = rms_cols(up32(x), gain_attn).astype(BF)
    qkv = dot_tn(h1, w_qkv).astype(BF)
    two, one = qkv[:, :384], qkv[:, 384:640]
    other, pieces[0] = after(swap(qkv[:, 640:1024], "cy"), pieces[0])
    two = jnp.stack([two, other])
    other, pieces[1] = after(swap(qkv[:, 1024:], "cy"), pieces[1])
    one = jnp.stack([one, other])
    blocks = lambda v: v.reshape(2 * nb, BLK, v.shape[-1])
    gather = lambda v: lax.all_gather(v, "cz", axis=0, tiled=True).reshape(NBLK, BLK, v.shape[-1])
    kv2, q2 = gather(two[:, :, :256]), blocks(two[:, :, 256:])
    kv1, q1 = gather(one[:, :, :128]), blocks(one[:, :, 128:])
    tab, lo, oo = plan(deal_table, seg_ids[0], ctx, nb)
    bias2, bias1 = bias_tables(my_table)
    w_early = jnp.concatenate([w_qkv[:, 256:640], w_qkv[:, 896:]], axis=1)
    w_late = jnp.concatenate([w_qkv[:, :256], w_qkv[:, 640:896]], axis=1)
    kv2, w_early, w_late = after(kv2, w_early, w_late)
    att2, lse2 = attn_fwd(False, tab, kv2, q2, *bias2, lo, oo)
    kv1, att2 = after(kv1, att2)
    att1, lse1 = attn_fwd(True, tab, kv1, q1, *bias1, lo, oo)
    halves2, halves1 = att2.reshape(2, rows, 128), att1.reshape(2, rows, 128)
    halves1, pair2, *far_w = after(halves1, swap(halves2[1], "cy"), *far_w, *pieces)
    far_w = far_w[:2] + [jnp.concatenate(far_w[2:])]
    att_rows = jnp.concatenate([halves2[0], halves1[0], pair2, swap(halves1[1], "cy")], axis=1)
    core_w = [swap(w, "fc") for w in own_w]
    last_w = [swap(w, "fc") for w in far_w]
    weights = list(zip(own_w, core_w, far_w, last_w))

    mid = up32(x) + dot_nt(w_o, att_rows)
    h2 = rms_cols(mid, gain_ffn).astype(BF)

    def split_ffn(v):
        v = v.reshape(steps, 2, -1, v.shape[1])
        flat_rows = lambda u: u.reshape(-1, u.shape[-1])
        even, odd = flat_rows(v[:, 0]), flat_rows(v[:, 1])
        return pick_half(par, even, odd), pick_half(par, odd, even)

    o_far = ffn_pair(h2, dy, *[w[2:] for w in weights])
    total = mid
    for r in (2, 3):
        total = total + dot_nn(weights[2][r], o_far[r - 2])
    fold = lambda o, k: up32(o[6 + k]) + up32(swap(o[9 + k], "fc"))
    far_g = [fold(o_far, k) for k in range(3)]
    cut = 2 * width // 3 // 16 * 16
    gate_far = far_g[0].astype(BF)
    to_x = [gate_far[:cut], gate_far[cut:], far_g[1].astype(BF)]
    keep_d, send_d = split_ffn(far_g[2])
    h2, total, keep_d, send_d, *to_x = after(h2, total, keep_d.astype(BF), send_d.astype(BF), *to_x)
    far_d = swap(send_d, "cy")
    gate_a, gate_b, far_up = [swap(g, "fx") for g in to_x]
    o_near = ffn_pair(h2, dy, *[w[:2] for w in weights])
    *o_near, far_d, gate_a = after(*o_near, far_d, gate_a)
    far_d = swap((up32(keep_d) + up32(far_d)).astype(BF), "fx")
    near_g = [fold(o_near, k) for k in range(3)]
    keep_d, send_d = split_ffn(near_g[2])
    near_d = swap(send_d.astype(BF), "cy")
    d_lists = [o_near[2], o_near[3], o_far[2], o_far[3], o_near[4], o_near[5], o_far[4], o_far[5]]
    w_lists = list(weights[0]) + list(weights[1])
    d_mid, d_branch, d_att, g_gain_ffn = ffn_back(d_lists, w_lists, mid, dy, gain_ffn, w_o)
    for r in (0, 1):
        total = total + dot_nn(weights[2][r], o_near[r])
    layer_out = jnp.transpose(total.astype(BF)).reshape(layer_in.shape)

    do1 = blocks(jnp.stack([d_att[:, 128:256], swap(d_att[:, 384:], "cy")]))
    do2 = blocks(jnp.stack([d_att[:, :128], swap(d_att[:, 256:384], "cy")]))
    do1, do2, far_d, near_d, far_gate = after(do1, do2, far_d, near_d, jnp.concatenate([gate_a, gate_b]))
    half_d = (keep_d + up32(near_d) + up32(far_d)).astype(BF)
    scatter = lambda v, dim: lax.psum_scatter(v, "cz", scatter_dimension=dim, tiled=True)
    half_d = lax.psum(half_d, "cz")
    keep_gate, send = split_ffn(near_g[0] + up32(far_gate))
    recv_gate = swap(send.astype(BF), "cy")
    dq1, dkv1, gt1, gz1 = attn_bwd(True, tab, kv1, q1, do1, att1, *bias1, lo, oo, lse1)
    dkv1, dq1, recv_gate, far_up = after(dkv1, dq1, recv_gate, far_up)
    dkv1 = scatter(dkv1.reshape(GROUP, 128), 0)
    half_gate = (keep_gate + up32(recv_gate)).astype(BF)
    piece_gate = scatter(half_gate, 0)
    keep_up, send = split_ffn(near_g[1] + up32(far_up))
    recv_up = swap(send.astype(BF), "cy")
    do2, far_up = after(do2, far_up)
    dq2, dkv2, gt2, gz2 = attn_bwd(False, tab, kv2, q2, do2, att2, *bias2, lo, oo, lse2)
    dkv2, dq2, dkv1, recv_up, piece_gate, half_d = after(dkv2, dq2, dkv1, recv_up, piece_gate, half_d)
    dkv2 = scatter(dkv2.reshape(GROUP, 256), 0)
    piece_up = scatter((keep_up + up32(recv_up)).astype(BF), 0)
    f_here = lax.axis_index("fx") * 2 + lax.axis_index("fc")

    def fold_attn(g, *counts):
        blocks = g.reshape(shards, share, g.shape[1])
        away = lambda r: lax.dynamic_index_in_dim(blocks, f_here ^ r, keepdims=False)
        near = up32(away(0)) + up32(swap(away(1), "fc"))
        far = (up32(away(2)) + up32(swap(away(3), "fc"))).astype(BF)
        own = near + up32(swap(far, "fx"))
        at, swapped = 0, []
        for count in counts:
            mid_at = at + count // 2
            swapped += [own[:, mid_at : at + count], own[:, at:mid_at]]
            at += count
        if at < own.shape[1]:
            swapped.append(own[:, at:])
        own = pick_half(par, own, jnp.concatenate(swapped, axis=1))
        return jnp.pad(own, ((0, (-share) % 64), (0, 0)))

    dq1, dq2 = dq1.reshape(2, rows, 128), dq2.reshape(2, rows, 128)
    early = [dq2[0], dkv1[:rows], dq1[0]] + [swap(v, "cy") for v in (dq2[1], dkv1[rows:], dq1[1])]
    d_part, g_early = in_part(jnp.concatenate(early, axis=1), w_early, h1)
    g_out = dot_nn(d_branch, att_rows).astype(BF)
    g_early = jnp.concatenate([g_early, g_out], axis=1)
    g_bias = bias_grads(gt2, gz2, gt1, gz1, table.shape[0])
    zero = jnp.zeros_like(g_bias)
    g_bias = jnp.concatenate([pick_half(par, g_bias, zero), pick_half(par, zero, g_bias)], axis=1)
    spare = jnp.pad(g_bias.reshape(shards, bias_rows, HEADS),
                    ((0, 0), (0, share - bias_rows), (2, 126 - HEADS))).reshape(width, 128)
    spare = jnp.where(jnp.arange(128)[None, :] == 1, g_gain_ffn, spare)
    dkv2, d_part, spare, g_early = after(
        dkv2, d_part, spare, fold_attn(g_early, 768, 512))
    late = jnp.concatenate([dkv2[:rows], swap(dkv2[rows:], "cy")], axis=1)
    def whole(half, other):
        both = [v.reshape(steps, 1, -1, v.shape[-1]) for v in (half, other)]
        both = jnp.concatenate([pick_half(par, *both), pick_half(par, *both[::-1])], axis=1)
        return up32(both.reshape(-1, half.shape[-1]))

    in_grad, g_late = in_back(late, w_late, d_part, x, h1, gain_attn, d_mid, spare)
    in_grad = jnp.transpose(in_grad).reshape(layer_in.shape)
    g_late, g_early, half_d, piece_up = after(g_late, g_early, half_d, piece_up)
    last = lax.all_gather(jnp.stack([piece_gate, piece_up]), ("cz", "cy"), axis=1, tiled=True)
    other_d = swap(half_d, "cy")
    g_late = up32(ctx_gather(ctx_scatter(fold_attn(g_late, 512), bits), bits)[:share])
    g_early = up32(ctx_gather(ctx_scatter(g_early, bits), bits)[:share])
    grad_down_t, grad_gate, grad_up = whole(half_d, other_d), up32(last[0]), up32(last[1])
    cols = lambda g, *starts: jnp.concatenate([g[:, a : a + HDIM] for a in starts], axis=1)
    k, v = lambda p: cols(g_late, 256 * p, 256 * p + 64), lambda p: cols(g_late, 256 * p + 128, 256 * p + 192)
    third = lambda p, a: cols(g_early, 384 * p + a)
    grad_key = jnp.concatenate([k(0), third(0, 128), k(1), third(1, 128)], axis=1)
    grad_value = jnp.concatenate([v(0), third(0, 192), v(1), third(1, 192)], axis=1)
    grad_query = cols(g_early, 0, 64, 256, 384, 448, 640)
    grad_out = jnp.transpose(cols(g_early, *[768 + a for a in (0, 64, 192, 256, 320, 448)]))
    rest = g_late[:, 512:]
    return (
        layer_out, in_grad, grad_query, grad_key, grad_value, grad_out, grad_gate, grad_up,
        jnp.transpose(grad_down_t), rest[:, 0], rest[:, 1], rest[:bias_rows, 2 : 2 + HEADS],
    )


def solution(mesh):
    devices = mesh.devices
    ctx_size, fsdp_size = mesh.shape["ctx"], mesh.shape["fsdp"]
    split = Mesh(devices.reshape(ctx_size // 2, 2, fsdp_size // 2, 2), ("cz", "cy", "fx", "fc"))
    cs, fs = ("cz", "cy"), ("fx", "fc")
    in_specs = (
        P(fs, cs, None), P(fs, cs, None), P(fs, None), P(fs, None), P(fs, None), P(None, fs),
        P(None, fs), P(None, fs), P(fs, None), P(fs), P(fs), P(fs, None), P(), P(fs, None),
    )
    out_specs = (
        P(fs, cs, None), P(fs, cs, None), P(fs, None), P(fs, None), P(fs, None), P(None, fs),
        P(None, fs), P(None, fs), P(fs, None), P(fs), P(fs), P(fs, None),
    )
    return jax.shard_map(
        on_device, mesh=split, in_specs=in_specs, out_specs=out_specs, check_vma=False
    )
```
